1024 devices in a mesh: shard: 64 (over y_lo, z), rep: 16 (over x, y_hi, core).
Axes of the slice: x: 4, y: 8 (y_hi: 2, y_lo: 4; y = y_hi * 4 + y_lo), z: 16, core: 2. Of those that a mesh axis runs over, the one named last changes fastest.
Arguments:
- images: bfloat16 [1024, 8, 16, 768], P(('shard', 'rep')), may hold values from -24 to 24
- cotangent: bfloat16 [1024, 8, 16, 1536], P(('shard', 'rep')), may hold values from -6 to 6
- depthwise_weight: bfloat16 [768, 49], P('shard'), may hold values from -0.875 to 0.875
- norm_gain: bfloat16 [768], P('shard'), may hold values from 0.5 to 1.5
- norm_bias: bfloat16 [768], P('shard'), may hold values from -3 to 3
- up_weight: bfloat16 [768, 1536], P('shard'), may hold values from -0.21875 to 0.21875
Outputs:
- grad_images: bfloat16 [1024, 8, 16, 768], P(('shard', 'rep'))
- grad_up: float32 [768, 1536], P('shard')
- grad_depthwise: float32 [768, 49], P('shard')
- grad_gain: float32 [768], P('shard')
- grad_bias: float32 [768], P('shard')
The draws below stay inside these ranges and needn't reach their ends.
All inputs are finite; a program needn't handle non-finite values.
Results may differ from the reference program's by a relative error of at most 0.0056.
Values may be sent and summed in bfloat16 or wider, within the bound.
A program may use at most 128 MiB of HBM per device.

```python
import math
import jax
import jax.numpy as jnp
from jax import lax

D = 768
HID = 1536
KS = 7
TH = 8
TW = 16
IMAGES = 1024


def spiked(drawn, stream_key, source, target, parts, factor):
    owner, partner = [(jnp.arange(drawn.shape[position]) // (drawn.shape[position] // parts)).reshape([-1 if axis == position else 1 for axis in range(drawn.ndim)]) for position in (source, target)]
    chosen = jax.random.permutation(stream_key, parts)[partner]
    strong = (owner == chosen) | (owner == (partner + parts // 2) % parts)
    return jnp.where(strong, factor * drawn, drawn)


def block_scale(own_key, dims, split, low, largest):
    level, own = 1.0, jax.random.fold_in(own_key, 6)
    for axis_at, shards_of in split:
        heights = jnp.exp(jax.random.uniform(jax.random.fold_in(own, axis_at), (shards_of,), jnp.float32, low / len(split), largest / len(split)))
        level = level * jnp.repeat(heights, dims[axis_at] // shards_of).reshape([-1 if axis == axis_at else 1 for axis in range(len(dims))])
    return level


def noise(rng, dims, width, most, pieces=(), held_as=jnp.bfloat16):
    entries = width * jax.random.normal(rng, dims, jnp.float32)
    if pieces:
        entries = entries * block_scale(rng, dims, pieces, -0.22, 0.18)
    return jnp.clip(entries, -most, most).astype(held_as)


def bell_draw_with(key, shape, scale, reach, cuts, heavy, dtype=jnp.bfloat16):
    entries = scale * jax.random.normal(key, shape, jnp.float32)
    if cuts:
        entries = entries * block_scale(key, shape, cuts, -0.22, 0.18)
    return jnp.clip(spiked(entries, jax.random.fold_in(key, 3), *heavy), -reach, reach).astype(dtype)


def setup_inputs(seed: int = 0) -> dict:
    seeds = jax.random.split(jax.random.key(seed), 7)
    images = bell_draw_with(seeds[0], (IMAGES, TH, TW, D), 1.0, 24.0, ((0, 1024),), (0, 3, 256, 6.0))
    cotangent = noise(seeds[1], (IMAGES, TH, TW, HID), 1.0, 6.0, ((0, 1024),))
    depthwise_weight = noise(seeds[2], (D, KS * KS), (KS * KS) ** -0.5, 0.875, ((0, 64),))
    norm_gain = jnp.clip(1.0 + 0.1 * jax.random.normal(seeds[3], (D,), jnp.float32), 0.5, 1.5).astype(jnp.bfloat16)
    norm_bias = noise(seeds[4], (D,), 0.5, 3.0, ((0, 64),))
    up_weight = noise(seeds[5], (D, HID), D ** -0.5, 0.21875, ((0, 64),))
    return dict(images=images, cotangent=cotangent, depthwise_weight=depthwise_weight, norm_gain=norm_gain, norm_bias=norm_bias, up_weight=up_weight)


norm_eps = 1e-06

def gelu_slope(inputs):
    cumulative = 0.5 * (1.0 + lax.erf(inputs * 0.7071067811865476))
    return cumulative + inputs * jnp.exp(-0.5 * inputs * inputs) * 0.3989422804014327

def pad_tile(source, margin):
    return jnp.pad(source, ((0, 0), (margin, margin), (margin, margin), (0, 0)))

def depthwise(source, kernel, extent):
    margin = extent // 2
    height, breadth = (source.shape[1], source.shape[2])
    padded = pad_tile(source, margin)
    running = jnp.zeros_like(source)
    for down_step in range(extent):
        for across in range(extent):
            running = running + padded[:, down_step:down_step + height, across:across + breadth, :] * kernel[:, down_step * extent + across]
    return running

def depthwise_back(grad_conv, kernel, extent):
    margin = extent // 2
    height, breadth = (grad_conv.shape[1], grad_conv.shape[2])
    padded = pad_tile(grad_conv, margin)
    running = jnp.zeros_like(grad_conv)
    for down_step in range(extent):
        for across in range(extent):
            top = 2 * margin - down_step
            left = 2 * margin - across
            running = running + padded[:, top:top + height, left:left + breadth, :] * kernel[:, down_step * extent + across]
    return running

def kernel_grad(source, grad_conv, extent):
    margin = extent // 2
    height, breadth = (source.shape[1], source.shape[2])
    padded = pad_tile(source, margin)
    columns = []
    for down_step in range(extent):
        for across in range(extent):
            columns.append(lax.optimization_barrier(jnp.sum(grad_conv * padded[:, down_step:down_step + height, across:across + breadth, :], axis=(0, 1, 2))))
    return jnp.stack(columns, axis=1)

def local_pass(x_tile, cot_tile, dw_weight, gain, bias, weight, extent):
    source = x_tile.astype(jnp.float32)
    kernel = dw_weight.astype(jnp.float32)
    conv_out = depthwise(source, kernel, extent)
    average = lax.optimization_barrier(jnp.mean(conv_out, axis=-1, keepdims=True))
    centered = conv_out - average
    inv_std = lax.rsqrt(lax.optimization_barrier(jnp.mean(centered * centered, axis=-1, keepdims=True)) + norm_eps)
    whitened = centered * inv_std
    gain_f = gain.astype(jnp.float32)
    normed = (whitened * gain_f + bias.astype(jnp.float32)).astype(jnp.bfloat16)
    depth = source.shape[-1]
    hidden = weight.shape[1]
    flattened = normed.reshape(-1, depth)
    pre_act = jnp.dot(flattened, weight, preferred_element_type=jnp.float32)
    grad_pre = (cot_tile.reshape(-1, hidden).astype(jnp.float32) * gelu_slope(pre_act)).astype(jnp.bfloat16)
    grad_normed = lax.dot_general(grad_pre, weight, (((1,), (1,)), ((), ())), preferred_element_type=jnp.float32).reshape(conv_out.shape)
    weight_term = lax.dot_general(flattened, grad_pre, (((0,), (0,)), ((), ())), preferred_element_type=jnp.float32)
    gain_term = lax.optimization_barrier(jnp.sum(grad_normed * whitened, axis=(0, 1, 2)))
    bias_term = lax.optimization_barrier(jnp.sum(grad_normed, axis=(0, 1, 2)))
    grad_white = grad_normed * gain_f
    grad_conv = inv_std * (grad_white - lax.optimization_barrier(jnp.mean(grad_white, axis=-1, keepdims=True)) - whitened * lax.optimization_barrier(jnp.mean(grad_white * whitened, axis=-1, keepdims=True)))
    kernel_term = kernel_grad(source, grad_conv, extent)
    grad_input = depthwise_back(grad_conv, kernel, extent).astype(jnp.bfloat16)
    return (grad_input, weight_term, kernel_term, gain_term, bias_term)

def reference(images, cotangent, depthwise_weight, norm_gain, norm_bias, up_weight):

    def accumulate(totals, slices):
        x_tile, cot_tile = slices
        grad_input, weight_term, kernel_term, gain_term, bias_term = local_pass(x_tile[None], cot_tile[None], depthwise_weight, norm_gain, norm_bias, up_weight, KS)
        return ((totals[0] + weight_term, totals[1] + kernel_term, totals[2] + gain_term, totals[3] + bias_term), grad_input[0])
    start_sums = (jnp.zeros((D, HID), jnp.float32), jnp.zeros((D, KS * KS), jnp.float32), jnp.zeros((D,), jnp.float32), jnp.zeros((D,), jnp.float32))
    summed, grad_images = lax.scan(accumulate, start_sums, (images, cotangent))
    factor = 1.0 / math.sqrt(IMAGES * TH * TW)
    return (grad_images, summed[0] * factor, summed[1] * factor, summed[2] * factor, summed[3] * factor)
```

```python
import functools
import math

import jax
import jax.numpy as jnp
from jax import lax
from jax.experimental import pallas as pl
from jax.experimental.pallas import tpu as pltpu
from jax.sharding import PartitionSpec as P

KS = 7
EPS = 1e-06
F32 = jnp.float32
BF16 = jnp.bfloat16
MESH = pl.DeviceIdType.MESH

NX, NYL, NYH, NZ, NC = 4, 4, 2, 16, 2
NY = NYL * NYH
QUAD = 4
CH = 6


def gelu_slope(v):
    cumulative = 0.5 * (1.0 + lax.erf(v * 0.7071067811865476))
    return cumulative + v * jnp.exp(-0.5 * v * v) * 0.3989422804014327


def kernel(
    factor,
    img_ref, cot_ref, wl_ref,
    gi_ref, gu_ref, sm_ref,
    zbuf, W, S, kT, xp, gp, cv, istd, N, NT, ctr, pre, G, GN, GNr,
    Pf, Pb, F, RB, RF, TB, SX, SXb, RY, SY, K, Kt, Kf, Kb, RK, KS_, ZSf, ZS, RZ, FIN, PC,
    s_z, r_z, s_g2, r_g2, s_wa, r_wa, s_wb, r_wb, s_c, r_c,
    s_m1, r_m1, s_m2, r_m2, s_m3, r_m3, s_y, r_y, s_k, r_k, s_z2, r_z2, s_r1, r_r1, s_r2, r_r2,
):
    s = lax.axis_index("shard")
    r = lax.axis_index("rep")
    yl, z = lax.div(s, NZ), lax.rem(s, NZ)
    x = lax.div(r, NYH * NC)
    yh = lax.rem(lax.div(r, NC), NYH)
    core = lax.rem(r, NC)
    y = yh * NYL + yl
    sgn = 1 - 2 * core
    zq, zr = lax.div(z, QUAD), lax.rem(z, QUAD)
    source = zq == x

    def dev(x_, y_, z_, c_):
        return (
            lax.rem(y_, NYL) * NZ + z_,
            x_ * (NYH * NC) + lax.div(y_, NYL) * NC + c_,
        )

    def dz(k):
        return dev(x, y, lax.rem(z + k, NZ), core)

    def dxy(dx, dy):
        return dev(lax.rem(x + dx + 2 * NX, NX), lax.rem(y + dy + 2 * NY, NY), z, core)

    sib = dev(x, y, z, 1 - core)

    def rcopy(src, dst, ss, rs, to):
        return pltpu.make_async_remote_copy(
            src_ref=src, dst_ref=dst, send_sem=ss, recv_sem=rs, device_id=to, device_id_type=MESH
        )

    barrier = pltpu.get_barrier_semaphore()

    def hello(to):
        pl.semaphore_signal(barrier, inc=1, device_id=to, device_id_type=MESH)

    @pl.loop(1, NZ)
    def _(k):
        hello(dz(k))

    @pl.loop(1, NX * NY)
    def _(k):
        hello(dxy(lax.div(k, NY), lax.rem(k, NY)))

    hello(sib)
    hello(dev(x, lax.rem(y + NYL, NY), z, 1 - core))
    pl.semaphore_wait(barrier, (NZ - 1) + (NX * NY - 1) + 2)

    def z_send(k):
        return rcopy(wl_ref.at[core], zbuf.at[zr], s_z.at[k - 1], r_z.at[zr], dz(k))

    @pl.when(source)
    def _():
        @pl.loop(1, NZ)
        def _(k):
            z_send(k).start()

    half_own = pl.ds(pl.multiple_of(core * 768, 128), 768)
    half_sib = pl.ds(pl.multiple_of((1 - core) * 768, 128), 768)
    cot_send = rcopy(cot_ref.at[:, half_sib], ctr, s_c.at[0], r_c.at[0], sib)
    cot_send.start()

    @pl.when(source)
    def _():
        zbuf[zr] = wl_ref[core]

    zero_edge = jnp.zeros((8, 8, 128), F32)
    for ck in range(CH):
        xp[ck, :, 0:8, :] = zero_edge
        xp[ck, :, 24:32, :] = zero_edge
        gp[ck, :, 0:8, :] = zero_edge
        gp[ck, :, 24:32, :] = zero_edge
        xp[ck, :, 8:24, :] = img_ref[:, :, ck * 128 : (ck + 1) * 128].astype(F32)
    K[...] = jnp.zeros_like(K)
    ZSf[...] = jnp.zeros_like(ZSf)

    for j in range(QUAD):
        @pl.when(jnp.logical_not(jnp.logical_and(source, zr == j)))
        def _():
            rcopy(wl_ref.at[core], zbuf.at[j], s_z.at[0], r_z.at[j], sib).wait_recv()

    rows = lax.broadcasted_iota(jnp.int32, (48, 64), 0)
    cols = lax.broadcasted_iota(jnp.int32, (48, 64), 1)
    pick48 = jnp.where(rows // 12 * 16 + rows % 12 == cols, 1.0, 0.0).astype(BF16)
    packed = jnp.dot(pick48, zbuf[...].reshape(64, 896), preferred_element_type=F32).astype(BF16)
    W[yl, x] = packed[:, :768]
    S[yl, x] = packed[:, 768:]

    def dy_of(i):
        return (0, 1, -1, 2 * sgn)[i]

    def small_send(k):
        return rcopy(
            S.at[yl, x], S.at[yl, x], s_g2.at[k - 1], r_g2.at[k - 1], dxy(k // 4, dy_of(k % 4))
        )

    smalls = [small_send(k) for k in range(1, 16)]
    for c in smalls:
        c.start()
    A, B = pl.ds(0, 384), pl.ds(384, 384)
    a2 = [
        rcopy(W.at[yl, x, :, A], W.at[yl, x, :, A], s_wa.at[i], r_wa.at[i], dxy(0, dy_of(i + 1)))
        for i in range(3)
    ]
    b2 = [
        rcopy(W.at[yl, x, :, B], W.at[yl, x, :, B], s_wb.at[i], r_wb.at[i], dxy(i + 1, 0))
        for i in range(3)
    ]
    for i in range(3):
        a2[i].start()
        b2[i].start()

    for c in smalls:
        c.wait_recv()
    for c in a2:
        c.wait_recv()
    xf = lax.rem(x + sgn + NX, NX)
    xb = lax.rem(x - sgn + NX, NX)
    to_f, to_b = dxy(sgn, 0), dxy(-sgn, 0)
    a3 = [
        rcopy(W.at[:, x, :, A], W.at[:, x, :, A], s_wa.at[3], r_wa.at[3], to_f),
        rcopy(W.at[:, x, :, A], W.at[:, x, :, A], s_wa.at[4], r_wa.at[4], to_b),
    ]
    a3[0].start()
    a3[1].start()
    for c in b2:
        c.wait_recv()
    b3 = [
        rcopy(W.at[yl, :, :, B], W.at[yl, :, :, B], s_wb.at[3 + i], r_wb.at[3 + i], dxy(0, dy_of(i + 1)))
        for i in range(3)
    ]
    for c in b3:
        c.start()
    a3_fwd = rcopy(W.at[:, xb, :, A], W.at[:, xb, :, A], s_wa.at[5], r_wa.at[5], to_f)

    kcols = jnp.transpose(S[...].reshape(768, 128).astype(F32))
    for ck in range(CH):
        kT[ck] = kcols[:64, ck * 128 : (ck + 1) * 128]

    a3[0].wait_recv()
    a3_fwd.start()

    @pl.loop(0, CH)
    def _(ck):
        acc = [jnp.zeros((16, 128), F32) for _ in range(8)]
        for b in range(KS):
            taps = [kT[ck, pl.ds(a * KS + b, 1), :] for a in range(KS)]
            for row in range(8):
                xs = xp[ck, row, pl.ds(5 + b, 16), :]
                for a in range(KS):
                    h = row - a + 3
                    if 0 <= h < 8:
                        acc[h] = acc[h] + xs * taps[a]
        for h in range(8):
            cv[ck, h] = acc[h]

    @pl.loop(0, 8)
    def _(h):
        v = [cv[ck, h] for ck in range(CH)]
        total = v[0]
        for ck in range(1, CH):
            total = total + v[ck]
        avg = jnp.sum(total, axis=-1, keepdims=True) * (1.0 / 768)
        v = [u - avg for u in v]
        total = v[0] * v[0]
        for ck in range(1, CH):
            total = total + v[ck] * v[ck]
        inv = lax.rsqrt(jnp.sum(total, axis=-1, keepdims=True) * (1.0 / 768) + EPS)
        istd[h] = jnp.broadcast_to(inv, (16, 128))
        for ck in range(CH):
            w = v[ck] * inv
            cv[ck, h] = w
            N[core, pl.ds(pl.multiple_of(h * 16, 16), 16), ck * 128 : (ck + 1) * 128] = (
                w * kT[ck, 49:50, :] + kT[ck, 50:51, :]
            ).astype(BF16)

    n_send = rcopy(N.at[core], N.at[core], s_c.at[1], r_c.at[1], sib)
    n_send.start()
    cot_send.wait_recv()
    n_send.wait_recv()
    NT[...] = jnp.transpose(N[...].reshape(256, 768).astype(F32)).astype(BF16)

    def pointwise(cols, waits):
        for c in waits:
            c.wait_recv()
        pre[:, cols] = jnp.dot(
            N[...].reshape(256, 768), W[:, :, :, cols].reshape(768, 384), preferred_element_type=F32
        )

    pointwise(slice(384, 768), b3)
    pointwise(slice(0, 384), [a3[1], a3_fwd])

    @pl.loop(0, 8)
    def _(i):
        at = pl.ds(pl.multiple_of(i * 16, 16), 16)
        slope = gelu_slope(pre[pl.ds(pl.multiple_of(core * 128 + i * 16, 16), 16), :])
        G[core, at, :] = (cot_ref[at, half_own].astype(F32) * slope).astype(BF16)
        slope = gelu_slope(pre[pl.ds(pl.multiple_of((1 - core) * 128 + i * 16, 16), 16), :])
        G[1 - core, at, :] = (ctr[at, :].astype(F32) * slope).astype(BF16)

    def m1(j, q):
        return rcopy(Pb.at[q, lax.rem(x + 2, NX)], F.at[j], s_m1.at[j], r_m1.at[j], to_f)

    def m2(j, q):
        return rcopy(Pb.at[q, xb], RB.at[j], s_m2.at[j], r_m2.at[j], to_b)

    def m3(j):
        return rcopy(TB.at[j], RF.at[j], s_m3.at[j], r_m3.at[j], to_f)

    order = (2, 3, 1, 0)
    pieces = [(j, lax.rem(yl + j, NYL)) for j in order]
    for j, q in pieces:
        part = jnp.dot(
            NT[pl.ds(pl.multiple_of(q * 192, 64), 192), :], G[...].reshape(256, 768),
            preferred_element_type=F32,
        ).reshape(QUAD, 48, 768)
        Pf[q] = part
        Pb[q] = part.astype(BF16)
        m1(j, q).start()
        m2(j, q).start()

    GN[...] = lax.dot_general(
        G[...].reshape(256, 768), W[...].reshape(768, 768), (((1,), (1,)), ((), ())),
        preferred_element_type=F32,
    ).reshape(2, 128, 768)
    gn_send = rcopy(GN.at[1 - core], GNr, s_c.at[2], r_c.at[2], sib)
    gn_send.start()

    def forward_m3(j, q):
        m1(j, q).wait_recv()
        TB[j] = (F[j].astype(F32) + Pf[q, xf]).astype(BF16)
        m3(j).start()

    for j, q in pieces:
        forward_m3(j, q)

    gn_send.wait_recv()

    def ln_back(h, carry):
        at = pl.ds(pl.multiple_of(h * 16, 16), 16)
        sums_g, sums_b = carry
        gn = [
            GN[core, at, ck * 128 : (ck + 1) * 128] + GNr[at, ck * 128 : (ck + 1) * 128]
            for ck in range(CH)
        ]
        wh = [cv[ck, h] for ck in range(CH)]
        sums_b = [a + g for a, g in zip(sums_b, gn)]
        sums_g = [a + g * w for a, g, w in zip(sums_g, gn, wh)]
        gw = [g * kT[ck, 49:50, :] for ck, g in enumerate(gn)]
        t1, t2 = gw[0], gw[0] * wh[0]
        for ck in range(1, CH):
            t1 = t1 + gw[ck]
            t2 = t2 + gw[ck] * wh[ck]
        m_1 = jnp.sum(t1, axis=-1, keepdims=True) * (1.0 / 768)
        m_2 = jnp.sum(t2, axis=-1, keepdims=True) * (1.0 / 768)
        inv = istd[h]
        for ck in range(CH):
            gp[ck, h, 8:24, :] = inv * (gw[ck] - m_1 - wh[ck] * m_2)
        return sums_g, sums_b

    zeros = [jnp.zeros((16, 128), F32) for _ in range(CH)]
    sums_g, sums_b = lax.fori_loop(0, 8, ln_back, (zeros, zeros))
    for ck in range(CH):
        K[ck, 49:50, :] = jnp.sum(sums_g[ck], axis=0, keepdims=True)
        K[ck, 50:51, :] = jnp.sum(sums_b[ck], axis=0, keepdims=True)

    @pl.loop(0, CH)
    def _(ck):
        g = [gp[ck, h, 8:24, :] for h in range(8)]
        for b in range(KS):
            acc = [None] * KS
            for row in range(8):
                xs = xp[ck, row, pl.ds(5 + b, 16), :]
                for a in range(KS):
                    h = row - a + 3
                    if 0 <= h < 8:
                        t = xs * g[h]
                        acc[a] = t if acc[a] is None else acc[a] + t
            for a in range(KS):
                K[ck, a * KS + b : a * KS + b + 1, :] = jnp.sum(acc[a], axis=0, keepdims=True)

    for ck in range(CH):
        Kt[ck * 128 : (ck + 1) * 128, :] = jnp.transpose(K[ck])
    kt = Kt[...].reshape(NYL, QUAD, 48, 128)
    Kf[...] = kt
    Kb[...] = kt.astype(BF16)

    def small_out(k):
        qx, ql = lax.rem(x + k // 4, NX), lax.rem(yl + k % 4, NYL)
        return rcopy(
            Kb.at[ql, qx], RK.at[k - 1], s_k.at[k - 1], r_k.at[k - 1], dev(qx, yh * NYL + ql, z, core)
        )

    outs = [small_out(k) for k in range(1, 16)]
    for c in outs:
        c.start()

    def y_send(j, q, d):
        y_to = lax.rem(y + d, NY)
        cols = pl.ds(pl.multiple_of(lax.div(y_to, NYL) * 384, 128), 384)
        return rcopy(SXb.at[q, :, cols], RY.at[d], s_y.at[d], r_y.at[d], dxy(0, d))

    for j, q in pieces:
        m2(j, q).wait_recv()
        m3(j).wait_recv()
        total = Pf[q, x] + RB[j].astype(F32) + RF[j].astype(F32)
        SXb[q] = total.astype(BF16)
        for d in (j, j + 4):
            if d:
                y_send(j, q, d).start()
        if j == 0:
            SX[...] = total

    @pl.loop(0, CH)
    def _(ck):
        acc = [jnp.zeros((16, 128), F32) for _ in range(8)]
        for b in range(KS):
            taps = [kT[ck, pl.ds(a * KS + b, 1), :] for a in range(KS)]
            for row in range(8):
                gs = gp[ck, row, pl.ds(11 - b, 16), :]
                for a in range(KS):
                    h = row + a - 3
                    if 0 <= h < 8:
                        acc[h] = acc[h] + gs * taps[a]
        lanes = pl.ds(pl.multiple_of(ck * 128, 128), 128)
        for h in range(8):
            gi_ref[h, :, lanes] = acc[h].astype(BF16)

    for c in outs:
        c.wait_recv()
    ksum = Kf[yl, x]
    for k in range(15):
        ksum = ksum + RK[k].astype(F32)
    KS_[...] = ksum
    own_cols = pl.ds(pl.multiple_of(yh * 384, 128), 384)
    for j, q in pieces:
        for d in (j, j + 4):
            if d:
                y_send(j, q, d).wait_recv()
    ysum = SX[:, own_cols]
    for d in range(1, NY):
        ysum = ysum + RY[d].astype(F32)
    SY[...] = ysum
    for j in range(QUAD):
        ZSf[j, 0:12, 0:384] = SY[12 * j : 12 * j + 12, :]
        ZSf[j, 0:12, 384:512] = KS_[12 * j : 12 * j + 12, :]
    ZS[...] = ZSf[...].astype(BF16)

    def z2_send(j):
        return rcopy(
            ZS.at[j], RZ.at[z], s_z2.at[j], r_z2.at[z], dev(x, y, x * QUAD + j, core)
        )

    for j in range(QUAD):
        @pl.when(x * QUAD + j != z)
        def _():
            z2_send(j).start()

    p = yh * NC + core

    def r1_send(i):
        return rcopy(FIN, PC.at[p], s_r1.at[i - 1], r_r1, dxy(i, 0))

    @pl.when(source)
    def _():
        RZ[z] = ZS[zr]

        @pl.loop(1, NZ)
        def _(k):
            frm = lax.rem(z + k, NZ)
            rcopy(ZS.at[0], RZ.at[frm], s_z2.at[0], r_z2.at[frm], sib).wait_recv()

        total = RZ[0].astype(F32)
        for k in range(1, NZ):
            total = total + RZ[k].astype(F32)
        FIN[...] = total * factor
        for i in range(1, NX):
            r1_send(i).start()
        PC[p] = total * factor

    @pl.when(jnp.logical_not(source))
    def _():
        r1_send(1).wait_recv()

    def r2_send(k):
        yh_to = (yh, 1 - yh)[k // 2]
        c_to = (core, 1 - core)[k % 2]
        return rcopy(PC.at[p], PC.at[p], s_r2.at[k - 1], r_r2.at[k - 1], dev(x, yh_to * NYL + yl, z, c_to))

    r2 = [r2_send(k) for k in range(1, 4)]
    for c in r2:
        c.start()
    for c in r2:
        c.wait_recv()
    for q in range(4):
        at = (q % NC) * 768 + (q // NC) * 384
        gu_ref[:, at : at + 384] = PC[q, 0:12, 0:384]
    sm_ref[...] = (PC[0, 0:12, 384:] + PC[1, 0:12, 384:]) + (PC[2, 0:12, 384:] + PC[3, 0:12, 384:])

    @pl.when(source)
    def _():
        @pl.loop(1, NZ)
        def _(k):
            z_send(k).wait_send()

        for i in range(1, NX):
            r1_send(i).wait_send()

    for c in [cot_send, n_send, gn_send, a3_fwd] + smalls + a2 + b2 + a3 + b3 + outs + r2:
        c.wait_send()
    for j, q in pieces:
        m1(j, q).wait_send()
        m2(j, q).wait_send()
        m3(j).wait_send()
        for d in (j, j + 4):
            if d:
                y_send(j, q, d).wait_send()
    for j in range(QUAD):
        @pl.when(x * QUAD + j != z)
        def _():
            z2_send(j).wait_send()


def body(images, cotangent, depthwise_weight, norm_gain, norm_bias, up_weight):
    pixels = (
        images.shape[0] * images.shape[1] * images.shape[2]
        * lax.axis_size("shard") * lax.axis_size("rep")
    )
    factor = 1.0 / math.sqrt(pixels)
    small = jnp.concatenate(
        [depthwise_weight, norm_gain[:, None], norm_bias[:, None], jnp.zeros((12, 77), BF16)], axis=1
    )
    block = jnp.stack(
        [jnp.concatenate([up_weight[:, :768], small], 1), jnp.concatenate([up_weight[:, 768:], small], 1)]
    )
    block = jnp.pad(block, ((0, 0), (0, 4), (0, 0)))
    dma = pltpu.SemaphoreType.DMA
    vm = lambda dtype, *shape: pltpu.VMEM(shape, dtype)
    gi, gu, sm = pl.pallas_call(
        functools.partial(kernel, factor),
        out_shape=(
            jax.ShapeDtypeStruct((8, 16, 768), BF16),
            jax.ShapeDtypeStruct((12, 1536), F32),
            jax.ShapeDtypeStruct((12, 128), F32),
        ),
        in_specs=[pl.BlockSpec(memory_space=pltpu.VMEM)] * 3,
        out_specs=[pl.BlockSpec(memory_space=pltpu.VMEM)] * 3,
        scratch_shapes=[
            vm(BF16, 4, 16, 896),
            vm(BF16, 4, 4, 48, 768),
            vm(BF16, 4, 4, 48, 128),
            vm(F32, CH, 64, 128),
            vm(F32, CH, 8, 32, 128),
            vm(F32, CH, 8, 32, 128),
            vm(F32, CH, 8, 16, 128),
            vm(F32, 8, 16, 128),
            vm(BF16, 2, 128, 768),
            vm(BF16, 768, 256),
            vm(BF16, 128, 768),
            vm(F32, 256, 768),
            vm(BF16, 2, 128, 768),
            vm(F32, 2, 128, 768),
            vm(F32, 128, 768),
            vm(F32, 4, 4, 48, 768),
            vm(BF16, 4, 4, 48, 768),
            vm(BF16, 4, 48, 768),
            vm(BF16, 4, 48, 768),
            vm(BF16, 4, 48, 768),
            vm(BF16, 4, 48, 768),
            vm(F32, 48, 768),
            vm(BF16, 4, 48, 768),
            vm(BF16, 8, 48, 384),
            vm(F32, 48, 384),
            vm(F32, CH, 128, 128),
            vm(F32, 768, 128),
            vm(F32, 4, 4, 48, 128),
            vm(BF16, 4, 4, 48, 128),
            vm(BF16, 15, 48, 128),
            vm(F32, 48, 128),
            vm(F32, 4, 16, 512),
            vm(BF16, 4, 16, 512),
            vm(BF16, 16, 16, 512),
            vm(F32, 16, 512),
            vm(F32, 4, 16, 512),
            dma((15,)), dma((4,)),
            dma((15,)), dma((15,)),
            dma((6,)), dma((6,)),
            dma((6,)), dma((6,)),
            dma((3,)), dma((3,)),
            dma((4,)), dma((4,)),
            dma((4,)), dma((4,)),
            dma((4,)), dma((4,)),
            dma((8,)), dma((8,)),
            dma((15,)), dma((15,)),
            dma((4,)), dma((16,)),
            dma((3,)), dma,
            dma((3,)), dma((3,)),
        ],
        compiler_params=pltpu.CompilerParams(
            collective_id=0, has_side_effects=True, vmem_limit_bytes=40 << 20
        ),
    )(images.reshape(8, 16, 768), cotangent.reshape(128, 1536), block)
    taps = KS * KS
    return (gi.reshape(images.shape), gu, sm[:, :taps], sm[:, taps], sm[:, taps + 1])


def solution(mesh):
    placed = (
        P(("shard", "rep"), None, None, None),
        P(("shard", "rep"), None, None, None),
        P("shard", None),
        P("shard"),
        P("shard"),
        P("shard", None),
    )
    return jax.shard_map(
        body,
        mesh=mesh,
        in_specs=placed,
        out_specs=(
            P(("shard", "rep"), None, None, None),
            P("shard", None),
            P("shard", None),
            P("shard"),
            P("shard"),
        ),
        check_vma=False,
    )
```

```python
import math

import jax
import jax.numpy as jnp
from jax import lax
from jax.experimental import pallas as pl
from jax.experimental.pallas import tpu as pltpu
from jax.sharding import PartitionSpec as P

KS = 7
EPS = 1e-06
F32 = jnp.float32
BF16 = jnp.bfloat16
MESH = pl.DeviceIdType.MESH

NX, NYL, NYH, NZ, NC = 4, 4, 2, 16, 2
NY = NYL * NYH
QUAD = 4
CH = 6


def gelu_slope(v):
    cumulative = 0.5 * (1.0 + lax.erf(v * 0.7071067811865476))
    return cumulative + v * jnp.exp(-0.5 * v * v) * 0.3989422804014327


def kernel(
    img_hbm, cot_hbm, dw_hbm, gain_hbm, bias_hbm, up_hbm,
    gi_hbm, gu_ref, sm_ref,
    gi_ref, imgv, upv, dwv, gnv, bsv, wlf, wl, zall,
    zbuf, W, S, kT, xp, gp, cv, istd, N, NT, Ct, pre, G, GN, GNr,
    Pf, Pb, F, RB, RF, TB, SX, SXb, RY, SY, K, Kt, Kf, Kb, RK, KS_, ZSf, ZS, RZ, FIN, PC,
    s_in, s_z, r_z, s_g2, r_g2, s_w, r_w, s_c, r_c,
    s_m, r_m1, r_m2, r_m3, s_y, r_y, s_k, r_k, s_z2, r_z2, s_r1, r_r1, s_r2, r_r2,
):
    s = lax.axis_index("shard")
    r = lax.axis_index("rep")
    yl, z = lax.div(s, NZ), lax.rem(s, NZ)
    x = lax.div(r, NYH * NC)
    yh = lax.rem(lax.div(r, NC), NYH)
    core = lax.rem(r, NC)
    y = yh * NYL + yl
    sgn = 1 - 2 * core
    zq, zr = lax.div(z, QUAD), lax.rem(z, QUAD)
    source = zq == x

    def dev(x_, y_, z_, c_):
        return (
            lax.rem(y_, NYL) * NZ + z_,
            x_ * (NYH * NC) + lax.div(y_, NYL) * NC + c_,
        )

    def dz(k):
        return dev(x, y, lax.rem(z + k, NZ), core)

    def dxy(dx, dy):
        return dev(lax.rem(x + dx + 2 * NX, NX), lax.rem(y + dy + 2 * NY, NY), z, core)

    sib = dev(x, y, z, 1 - core)
    far = dev(x, lax.rem(y + NYL, NY), z, 1 - core)

    def rcopy(src, dst, ss, rs, to):
        return pltpu.make_async_remote_copy(
            src_ref=src, dst_ref=dst, send_sem=ss, recv_sem=rs, device_id=to, device_id_type=MESH
        )

    def landed(ref, sem):
        rcopy(ref, ref, s_in.at[0], sem, sib).wait_recv()

    def left(ref, sem):
        rcopy(ref, ref, sem, s_in.at[0], sib).wait_send()

    def dy_of(i):
        return (0, 1, -1, 2 * sgn)[i]

    half_own = pl.ds(pl.multiple_of(core * 768, 128), 768)
    half_sib = pl.ds(pl.multiple_of((1 - core) * 768, 128), 768)

    barrier = pltpu.get_barrier_semaphore()

    def hello(to):
        pl.semaphore_signal(barrier, inc=1, device_id=to, device_id_type=MESH)

    @pl.when(source)
    def _():
        @pl.loop(1, NZ)
        def _(k):
            hello(dz(k))

    @pl.when(jnp.logical_not(source))
    def _():
        for j in range(QUAD):
            hello(dev(x, y, x * QUAD + j, core))

    loads = [
        pltpu.make_async_copy(src, dst, s_in.at[i])
        for i, (src, dst) in enumerate(
            [(up_hbm, upv), (dw_hbm, dwv), (gain_hbm, gnv), (bias_hbm, bsv), (img_hbm, imgv),
             (cot_hbm.at[:, half_own], Ct.at[core])]
        )
    ]
    for c in loads:
        c.start()
    for d in range(1, NY):
        hello(dxy(0, d))
    for dx in range(1, NX):
        for i in range(4):
            hello(dxy(-dx, -dy_of(i)))
    hello(sib)
    hello(far)

    wlf[...] = jnp.zeros_like(wlf)
    for c in loads[:4]:
        c.wait()
    wlf[0:12, 0:768] = upv[:, half_own].astype(F32)
    wlf[0:12, 768:817] = dwv[...].astype(F32)
    row12 = lax.broadcasted_iota(jnp.int32, (12, 12), 0)
    col12 = lax.broadcasted_iota(jnp.int32, (12, 12), 1)

    def column(v):
        return jnp.sum(jnp.where(row12 == col12, v[...].astype(F32), 0.0), axis=1, keepdims=True)

    lane = lax.broadcasted_iota(jnp.int32, (12, 128), 1)
    extra = jnp.where(lane == 49, column(gnv), jnp.where(lane == 50, column(bsv), 0.0))
    wlf[0:12, 768:896] = wlf[0:12, 768:896] + extra
    wl[...] = wlf[...].astype(BF16)
    pl.semaphore_wait(barrier, 25 + 11 * source.astype(jnp.int32))

    @pl.when(source)
    def _():
        @pl.loop(1, NZ)
        def _(k):
            rcopy(wl, zbuf.at[zr], s_z, r_z, dz(k)).start()

        zbuf[zr] = wl[...]

    cot_send = rcopy(cot_hbm.at[:, half_sib], Ct.at[core], s_c.at[0], r_c.at[0], sib)
    cot_send.start()

    zero_edge = jnp.zeros((8, 8, 128), F32)
    loads[4].wait()
    for ck in range(CH):
        xp[ck, :, 0:8, :] = zero_edge
        xp[ck, :, 24:32, :] = zero_edge
        gp[ck, :, 0:8, :] = zero_edge
        gp[ck, :, 24:32, :] = zero_edge
        xp[ck, :, 8:24, :] = imgv[:, :, ck * 128 : (ck + 1) * 128].astype(F32)
    K[...] = jnp.zeros_like(K)
    ZSf[...] = jnp.zeros_like(ZSf)
    loads[5].wait()

    @pl.when(source)
    def _():
        landed(zbuf.at[pl.ds(0, 3)], r_z)

    @pl.when(jnp.logical_not(source))
    def _():
        landed(zbuf, r_z)

    rows = lax.broadcasted_iota(jnp.int32, (48, 64), 0)
    cols = lax.broadcasted_iota(jnp.int32, (48, 64), 1)
    pick48 = jnp.where(rows // 12 * 16 + rows % 12 == cols, 1.0, 0.0).astype(BF16)
    packed = jnp.dot(pick48, zbuf[...].reshape(64, 896), preferred_element_type=F32)
    W[yl, x] = packed[:, :768].astype(BF16)
    slot = yl * QUAD + x
    S[slot] = (packed[0:24, 768:] + pltpu.roll(packed[24:48, 768:], 64, 1)).astype(BF16)

    for k in range(1, 16):
        rcopy(S.at[slot], S.at[slot], s_g2, r_g2, dxy(k // 4, dy_of(k % 4))).start()
    A, B = pl.ds(0, 384), pl.ds(384, 384)
    for i in range(1, 4):
        rcopy(W.at[yl, x, :, A], W.at[yl, x, :, A], s_w.at[0], r_w.at[0], dxy(0, dy_of(i))).start()
        rcopy(W.at[yl, x, :, B], W.at[yl, x, :, B], s_w.at[1], r_w.at[1], dxy(i, 0)).start()

    landed(W.at[0, pl.ds(0, 3), :, A], r_w.at[0])
    for i in range(1, 4):
        rcopy(W.at[:, x, :, A], W.at[:, x, :, A], s_w.at[2], r_w.at[2], dxy(i, 0)).start()
    landed(W.at[0, pl.ds(0, 3), :, B], r_w.at[1])
    for i in range(1, 4):
        rcopy(W.at[yl, :, :, B], W.at[yl, :, :, B], s_w.at[3], r_w.at[3], dxy(0, dy_of(i))).start()

    landed(S.at[pl.ds(0, 15)], r_g2)
    flat = S[...].astype(F32)
    other = pltpu.roll(flat.reshape(384, 128), 64, 1).reshape(16, 24, 128)
    kcols = jnp.transpose(jnp.concatenate([flat, other], axis=1).reshape(768, 128))
    for ck in range(CH):
        kT[ck] = kcols[:64, ck * 128 : (ck + 1) * 128]

    @pl.loop(0, CH)
    def _(ck):
        acc = [jnp.zeros((16, 128), F32) for _ in range(8)]
        for b in range(KS):
            taps = [kT[ck, pl.ds(a * KS + b, 1), :] for a in range(KS)]
            for row in range(8):
                xs = xp[ck, row, pl.ds(5 + b, 16), :]
                for a in range(KS):
                    h = row - a + 3
                    if 0 <= h < 8:
                        acc[h] = acc[h] + xs * taps[a]
        for h in range(8):
            cv[ck, h] = acc[h]

    @pl.loop(0, 8)
    def _(h):
        v = [cv[ck, h] for ck in range(CH)]
        total = v[0]
        for ck in range(1, CH):
            total = total + v[ck]
        avg = jnp.sum(total, axis=-1, keepdims=True) * (1.0 / 768)
        v = [u - avg for u in v]
        total = v[0] * v[0]
        for ck in range(1, CH):
            total = total + v[ck] * v[ck]
        inv = lax.rsqrt(jnp.sum(total, axis=-1, keepdims=True) * (1.0 / 768) + EPS)
        istd[h] = jnp.broadcast_to(inv, (16, 128))
        for ck in range(CH):
            w = v[ck] * inv
            cv[ck, h] = w
            N[core, pl.ds(pl.multiple_of(h * 16, 16), 16), ck * 128 : (ck + 1) * 128] = (
                w * kT[ck, 49:50, :] + kT[ck, 50:51, :]
            ).astype(BF16)

    n_send = rcopy(N.at[core], N.at[core], s_c.at[1], r_c.at[1], sib)
    n_send.start()

    def flip(c):
        NT[:, pl.ds(pl.multiple_of(c * 128, 128), 128)] = jnp.transpose(N[c].astype(F32)).astype(BF16)

    flip(core)
    n_send.wait_recv()
    flip(1 - core)
    cot_send.wait_recv()

    def pointwise(cols):
        pre[:, cols] = jnp.dot(
            N[...].reshape(256, 768), W[:, :, :, cols].reshape(768, 384), preferred_element_type=F32
        )

    landed(W.at[pl.ds(0, 3), :, :, A], r_w.at[2])
    pointwise(slice(0, 384))
    landed(W.at[pl.ds(0, 3), :, :, B], r_w.at[3])
    pointwise(slice(384, 768))

    @pl.loop(0, 8)
    def _(i):
        at = pl.ds(pl.multiple_of(i * 16, 16), 16)
        for c in range(2):
            slope = gelu_slope(pre[pl.ds(pl.multiple_of(c * 128 + i * 16, 16), 16), :])
            G[c, at, :] = (Ct[c, at, :].astype(F32) * slope).astype(BF16)

    xf = lax.rem(x + sgn + NX, NX)
    xb = lax.rem(x - sgn + NX, NX)
    to_f, to_b = dxy(sgn, 0), dxy(-sgn, 0)
    pieces = [(j, lax.rem(yl + j, NYL)) for j in (2, 3, 1, 0)]
    for j, q in pieces:
        part = jnp.dot(
            NT[pl.ds(pl.multiple_of(q * 192, 64), 192), :], G[...].reshape(256, 768),
            preferred_element_type=F32,
        ).reshape(QUAD, 48, 768)
        Pf[q] = part
        Pb[q] = part.astype(BF16)
        rcopy(Pb.at[q, lax.rem(x + 2, NX)], F.at[j], s_m.at[0], r_m1.at[j], to_f).start()
        rcopy(Pb.at[q, xb], RB.at[j], s_m.at[1], r_m2.at[j], to_b).start()

    GN[...] = lax.dot_general(
        G[...].reshape(256, 768), W[...].reshape(768, 768), (((1,), (1,)), ((), ())),
        preferred_element_type=F32,
    ).reshape(2, 128, 768)
    gn_send = rcopy(GN.at[1 - core], GNr, s_c.at[2], r_c.at[2], sib)
    gn_send.start()

    def forward_x(j, q):
        landed(F.at[j], r_m1.at[j])
        TB[j] = (F[j].astype(F32) + Pf[q, xf]).astype(BF16)
        rcopy(TB.at[j], RF.at[j], s_m.at[2], r_m3.at[j], to_f).start()

    def into_y(j, q):
        landed(RB.at[j], r_m2.at[j])
        landed(RF.at[j], r_m3.at[j])
        total = Pf[q, x] + RB[j].astype(F32) + RF[j].astype(F32)
        SXb[q] = total.astype(BF16)
        for d in (j, j + 4):
            if d:
                cols = pl.ds(pl.multiple_of(lax.div(lax.rem(y + d, NY), NYL) * 384, 128), 384)
                rcopy(SXb.at[q, :, cols], RY.at[d - 1], s_y, r_y, dxy(0, d)).start()
        if j == 0:
            SX[...] = total

    forward_x(*pieces[0])
    forward_x(*pieces[1])
    gn_send.wait_recv()

    def ln_back(h, carry):
        at = pl.ds(pl.multiple_of(h * 16, 16), 16)
        sums_g, sums_b = carry
        gn = [
            GN[core, at, ck * 128 : (ck + 1) * 128] + GNr[at, ck * 128 : (ck + 1) * 128]
            for ck in range(CH)
        ]
        wh = [cv[ck, h] for ck in range(CH)]
        sums_b = [a + g for a, g in zip(sums_b, gn)]
        sums_g = [a + g * w for a, g, w in zip(sums_g, gn, wh)]
        gw = [g * kT[ck, 49:50, :] for ck, g in enumerate(gn)]
        t1, t2 = gw[0], gw[0] * wh[0]
        for ck in range(1, CH):
            t1 = t1 + gw[ck]
            t2 = t2 + gw[ck] * wh[ck]
        m_1 = jnp.sum(t1, axis=-1, keepdims=True) * (1.0 / 768)
        m_2 = jnp.sum(t2, axis=-1, keepdims=True) * (1.0 / 768)
        inv = istd[h]
        for ck in range(CH):
            gp[ck, h, 8:24, :] = inv * (gw[ck] - m_1 - wh[ck] * m_2)
        return sums_g, sums_b

    zeros = [jnp.zeros((16, 128), F32) for _ in range(CH)]
    sums_g, sums_b = lax.fori_loop(0, 8, ln_back, (zeros, zeros))
    for ck in range(CH):
        K[ck, 49:50, :] = jnp.sum(sums_g[ck], axis=0, keepdims=True)
        K[ck, 50:51, :] = jnp.sum(sums_b[ck], axis=0, keepdims=True)
    forward_x(*pieces[2])
    forward_x(*pieces[3])

    def kernel_grad(ck):
        g = [gp[ck, h, 8:24, :] for h in range(8)]
        for b in range(KS):
            acc = [None] * KS
            for row in range(8):
                xs = xp[ck, row, pl.ds(5 + b, 16), :]
                for a in range(KS):
                    h = row - a + 3
                    if 0 <= h < 8:
                        t = xs * g[h]
                        acc[a] = t if acc[a] is None else acc[a] + t
            for a in range(KS):
                K[ck, a * KS + b : a * KS + b + 1, :] = jnp.sum(acc[a], axis=0, keepdims=True)

    pl.loop(0, CH // 2)(kernel_grad)
    into_y(*pieces[0])
    pl.loop(CH // 2, CH)(kernel_grad)

    for ck in range(CH):
        Kt[ck * 128 : (ck + 1) * 128, :] = jnp.transpose(K[ck])
    kt = Kt[...].reshape(16, 48, 128)
    kt = kt[:, :24] + pltpu.roll(kt[:, 24:].reshape(384, 128), 64, 1).reshape(16, 24, 128)
    Kf[...] = kt
    Kb[...] = kt.astype(BF16)
    for k in range(1, 16):
        qx, ql = lax.rem(x + k // 4, NX), lax.rem(yl + dy_of(k % 4) + NYL, NYL)
        rcopy(Kb.at[ql * QUAD + qx], RK.at[k - 1], s_k, r_k, dxy(k // 4, dy_of(k % 4))).start()

    for piece in pieces[1:]:
        into_y(*piece)

    landed(RK, r_k)
    ksum = Kf[slot]
    for k in range(15):
        ksum = ksum + RK[k].astype(F32)
    KS_[0:24, :] = ksum
    KS_[24:48, :] = pltpu.roll(ksum, 64, 1)
    landed(RY, r_y)
    ysum = SX[:, pl.ds(pl.multiple_of(yh * 384, 128), 384)]
    for d in range(NY - 1):
        ysum = ysum + RY[d].astype(F32)
    SY[...] = ysum
    for j in range(QUAD):
        ZSf[j, 0:12, 0:384] = SY[12 * j : 12 * j + 12, :]
        ZSf[j, 0:12, 384:512] = KS_[12 * j : 12 * j + 12, :]
    ZS[...] = ZSf[...].astype(BF16)
    for j in range(QUAD):
        @pl.when(x * QUAD + j != z)
        def _():
            rcopy(ZS.at[j], RZ.at[z], s_z2, r_z2, dev(x, y, x * QUAD + j, core)).start()

    @pl.loop(0, CH)
    def _(ck):
        acc = [jnp.zeros((16, 128), F32) for _ in range(8)]
        for b in range(KS):
            taps = [kT[ck, pl.ds(a * KS + b, 1), :] for a in range(KS)]
            for row in range(8):
                gs = gp[ck, row, pl.ds(11 - b, 16), :]
                for a in range(KS):
                    h = row + a - 3
                    if 0 <= h < 8:
                        acc[h] = acc[h] + gs * taps[a]
        lanes = pl.ds(pl.multiple_of(ck * 128, 128), 128)
        for h in range(8):
            gi_ref[h, :, lanes] = acc[h].astype(BF16)

    store = pltpu.make_async_copy(gi_ref, gi_hbm, s_in.at[4])
    store.start()

    p = yh * NC + core

    @pl.when(source)
    def _():
        RZ[z] = ZS[zr]
        landed(RZ.at[pl.ds(0, 15)], r_z2)
        total = RZ[0].astype(F32)
        for k in range(1, NZ):
            total = total + RZ[k].astype(F32)
        FIN[...] = total
        for i in range(1, NX):
            rcopy(FIN, PC.at[p], s_r1, r_r1, dxy(i, 0)).start()
        PC[p] = total

    @pl.when(jnp.logical_not(source))
    def _():
        landed(FIN, r_r1)

    for to in (sib, dxy(0, NYL), far):
        rcopy(PC.at[p], PC.at[p], s_r2, r_r2, to).start()
    landed(PC.at[pl.ds(0, 3)], r_r2)
    for q in range(4):
        at = (q % NC) * 768 + (q // NC) * 384
        gu_ref[:, at : at + 384] = PC[q, 0:12, 0:384]
    sm_ref[...] = (PC[0, 0:12, 384:] + PC[1, 0:12, 384:]) + (PC[2, 0:12, 384:] + PC[3, 0:12, 384:])

    @pl.when(source)
    def _():
        left(zall, s_z)
        left(PC.at[pl.ds(0, 3)], s_r1)
        left(ZS.at[pl.ds(0, 3)], s_z2)

    @pl.when(jnp.logical_not(source))
    def _():
        left(ZS, s_z2)

    store.wait()
    for c in (cot_send, n_send, gn_send):
        c.wait_send()
    left(S.at[pl.ds(0, 15)], s_g2)
    left(W.at[0, pl.ds(0, 3), :, A], s_w.at[0])
    left(W.at[0, pl.ds(0, 3), :, B], s_w.at[1])
    left(W.at[pl.ds(0, 3), :, :, A], s_w.at[2])
    left(W.at[pl.ds(0, 3), :, :, B], s_w.at[3])
    for i in range(3):
        left(TB, s_m.at[i])
    left(RY, s_y)
    left(RK, s_k)
    left(PC.at[pl.ds(0, 3)], s_r2)


def body(images, cotangent, depthwise_weight, norm_gain, norm_bias, up_weight):
    pixels = (
        images.shape[0] * images.shape[1] * images.shape[2]
        * lax.axis_size("shard") * lax.axis_size("rep")
    )
    factor = 1.0 / math.sqrt(pixels)
    dma = pltpu.SemaphoreType.DMA
    vm = lambda dtype, *shape: pltpu.VMEM(shape, dtype)
    gi, gu, sm = pl.pallas_call(
        kernel,
        out_shape=(
            jax.ShapeDtypeStruct((8, 16, 768), BF16),
            jax.ShapeDtypeStruct((12, 1536), F32),
            jax.ShapeDtypeStruct((12, 128), F32),
        ),
        in_specs=[pl.BlockSpec(memory_space=pltpu.HBM)] * 6,
        out_specs=[
            pl.BlockSpec(memory_space=pltpu.HBM),
            pl.BlockSpec(memory_space=pltpu.VMEM),
            pl.BlockSpec(memory_space=pltpu.VMEM),
        ],
        scratch_shapes=[
            vm(BF16, 8, 16, 768),
            vm(BF16, 8, 16, 768),
            vm(BF16, 12, 1536),
            vm(BF16, 12, 49),
            vm(BF16, 1, 12),
            vm(BF16, 1, 12),
            vm(F32, 16, 896),
            vm(BF16, 16, 896),
            vm(BF16, 15, 16, 896),
            vm(BF16, 4, 16, 896),
            vm(BF16, 4, 4, 48, 768),
            vm(BF16, 16, 24, 128),
            vm(F32, CH, 64, 128),
            vm(F32, CH, 8, 32, 128),
            vm(F32, CH, 8, 32, 128),
            vm(F32, CH, 8, 16, 128),
            vm(F32, 8, 16, 128),
            vm(BF16, 2, 128, 768),
            vm(BF16, 768, 256),
            vm(BF16, 2, 128, 768),
            vm(F32, 256, 768),
            vm(BF16, 2, 128, 768),
            vm(F32, 2, 128, 768),
            vm(F32, 128, 768),
            vm(F32, 4, 4, 48, 768),
            vm(BF16, 4, 4, 48, 768),
            vm(BF16, 4, 48, 768),
            vm(BF16, 4, 48, 768),
            vm(BF16, 4, 48, 768),
            vm(BF16, 4, 48, 768),
            vm(F32, 48, 768),
            vm(BF16, 4, 48, 768),
            vm(BF16, 7, 48, 384),
            vm(F32, 48, 384),
            vm(F32, CH, 128, 128),
            vm(F32, 768, 128),
            vm(F32, 16, 24, 128),
            vm(BF16, 16, 24, 128),
            vm(BF16, 15, 24, 128),
            vm(F32, 48, 128),
            vm(F32, 4, 16, 512),
            vm(BF16, 4, 16, 512),
            vm(BF16, 16, 16, 512),
            vm(F32, 16, 512),
            vm(F32, 4, 16, 512),
            dma((6,)),
            dma, dma,
            dma, dma,
            dma((4,)), dma((4,)),
            dma((3,)), dma((3,)),
            dma((3,)), dma((4,)), dma((4,)), dma((4,)),
            dma, dma,
            dma, dma,
            dma, dma,
            dma, dma,
            dma, dma,
        ],
        compiler_params=pltpu.CompilerParams(
            collective_id=0, has_side_effects=True, vmem_limit_bytes=58 << 20
        ),
    )(
        images.reshape(8, 16, 768), cotangent.reshape(128, 1536), depthwise_weight,
        norm_gain.reshape(1, 12), norm_bias.reshape(1, 12), up_weight,
    )
    taps = KS * KS
    sm = sm * factor
    return (gi.reshape(images.shape), gu * factor, sm[:, :taps], sm[:, taps], sm[:, taps + 1])


def solution(mesh):
    placed = (
        P(("shard", "rep"), None, None, None),
        P(("shard", "rep"), None, None, None),
        P("shard", None),
        P("shard"),
        P("shard"),
        P("shard", None),
    )
    return jax.shard_map(
        body,
        mesh=mesh,
        in_specs=placed,
        out_specs=(
            P(("shard", "rep"), None, None, None),
            P("shard", None),
            P("shard", None),
            P("shard"),
            P("shard"),
        ),
        check_vma=False,
    )
```

```python
import math

import jax
import jax.numpy as jnp
from jax import lax
from jax.experimental import pallas as pl
from jax.experimental.pallas import tpu as pltpu
from jax.sharding import PartitionSpec as P

KS = 7
EPS = 1e-06
F32 = jnp.float32
BF16 = jnp.bfloat16
MESH = pl.DeviceIdType.MESH

NX, NYL, NYH, NZ, NC = 4, 4, 2, 16, 2
NY = NYL * NYH
QUAD = 4
CH = 6


def gelu_slope(v):
    cumulative = 0.5 * (1.0 + lax.erf(v * 0.7071067811865476))
    return cumulative + v * jnp.exp(-0.5 * v * v) * 0.3989422804014327


def kernel(
    img_hbm, cot_hbm, dw_hbm, gain_hbm, bias_hbm, up_hbm,
    gi_ref, gu_ref, sm_ref,
    gip, order, imgv, upv, dwv, gnv, bsv, wlf, wl, zall,
    zbuf, W, S, kT, xp, gp, cv, istd, N, NT, Ct, pre, G, GN, GNr,
    Pf, Pb, F, RB, RF, TB, SX, SXb, RY, SY, K, Kt, Kf, Kb, RK, KS_, ZSf, ZS, RZ, FIN, PC,
    s_in, s_z, r_z, s_g2, r_g2, s_w, r_w, s_c, r_c,
    s_m, r_m1, r_m2, r_m3, s_y, r_y, s_k, r_k, s_z2, r_z2, s_r1, r_r1, s_r2, r_r2,
):
    s = lax.axis_index("shard")
    r = lax.axis_index("rep")
    yl, z = lax.div(s, NZ), lax.rem(s, NZ)
    x = lax.div(r, NYH * NC)
    yh = lax.rem(lax.div(r, NC), NYH)
    core = lax.rem(r, NC)
    y = yh * NYL + yl
    sgn = 1 - 2 * core
    zr = lax.div(z, QUAD)
    source = lax.rem(z, QUAD) == x

    def dev(x_, y_, z_, c_):
        return (
            lax.rem(y_, NYL) * NZ + z_,
            x_ * (NYH * NC) + lax.div(y_, NYL) * NC + c_,
        )

    def dz(k):
        return dev(x, y, lax.rem(z + k, NZ), core)

    def far_first(i):
        return 8 + lax.div(i + 1, 2) * (1 - 2 * lax.rem(i, 2))

    def dxy(dx, dy):
        return dev(lax.rem(x + dx + 2 * NX, NX), lax.rem(y + dy + 2 * NY, NY), z, core)

    sib = dev(x, y, z, 1 - core)
    far = dev(x, lax.rem(y + NYL, NY), z, 1 - core)

    def rcopy(src, dst, ss, rs, to):
        return pltpu.make_async_remote_copy(
            src_ref=src, dst_ref=dst, send_sem=ss, recv_sem=rs, device_id=to, device_id_type=MESH
        )

    def landed(ref, sem):
        rcopy(ref, ref, s_in.at[0], sem, sib).wait_recv()

    def left(ref, sem):
        rcopy(ref, ref, sem, s_in.at[0], sib).wait_send()

    def dy_of(i):
        return (0, 1, -1, 2 * sgn)[i]

    half_own = pl.ds(pl.multiple_of(core * 768, 128), 768)
    half_sib = pl.ds(pl.multiple_of((1 - core) * 768, 128), 768)

    barrier = pltpu.get_barrier_semaphore()

    def hello(to):
        pl.semaphore_signal(barrier, inc=1, device_id=to, device_id_type=MESH)

    @pl.when(source)
    def _():
        @pl.loop(0, NZ - 1)
        def _(i):
            hello(dz(far_first(i)))

    @pl.when(jnp.logical_not(source))
    def _():
        for j in range(QUAD):
            hello(dev(x, y, x + QUAD * j, core))

    loads = [
        pltpu.make_async_copy(src, dst, s_in.at[i])
        for i, (src, dst) in enumerate(
            [(up_hbm, upv), (dw_hbm, dwv), (gain_hbm, gnv), (bias_hbm, bsv), (img_hbm, imgv),
             (cot_hbm.at[:, half_own], Ct.at[core])]
        )
    ]
    for c in loads:
        c.start()
    for d in range(1, NY):
        hello(dxy(0, d))
    for dx in range(1, NX):
        for i in range(4):
            hello(dxy(-dx, -dy_of(i)))
    hello(sib)
    hello(far)

    wlf[...] = jnp.zeros_like(wlf)
    for c in loads[:4]:
        c.wait()
    wlf[0:12, 0:768] = upv[:, half_own].astype(F32)
    wlf[0:12, 768:817] = dwv[...].astype(F32)
    row12 = lax.broadcasted_iota(jnp.int32, (12, 12), 0)
    col12 = lax.broadcasted_iota(jnp.int32, (12, 12), 1)

    def column(v):
        return jnp.sum(jnp.where(row12 == col12, v[...].astype(F32), 0.0), axis=1, keepdims=True)

    lane = lax.broadcasted_iota(jnp.int32, (12, 128), 1)
    extra = jnp.where(lane == 49, column(gnv), jnp.where(lane == 50, column(bsv), 0.0))
    wlf[0:12, 768:896] = wlf[0:12, 768:896] + extra
    wl[...] = wlf[...].astype(BF16)
    pl.semaphore_wait(barrier, 25 + 11 * source.astype(jnp.int32))

    @pl.when(source)
    def _():
        @pl.loop(0, NZ - 1)
        def _(i):
            rcopy(wl, zbuf.at[zr], s_z, r_z, dz(far_first(i))).start()

        zbuf[zr] = wl[...]

    cot_send = rcopy(cot_hbm.at[:, half_sib], Ct.at[core], s_c.at[0], r_c.at[0], sib)
    cot_send.start()

    zero_edge = jnp.zeros((8, 8, 128), F32)
    place = lax.broadcasted_iota(jnp.int32, (8, 768), 1)
    block, inner = place // 48, place % 48
    channel = (block // QUAD * NZ + block % QUAD + QUAD * (inner // 12)) * 12 + inner % 12
    near = lax.broadcasted_iota(jnp.int32, (8, 768), 0)

    @pl.loop(0, 48)
    def _(i):
        at = pl.multiple_of(i * 16, 16)
        order[pl.ds(at, 16), :] = jnp.concatenate(
            [jnp.where(channel == near + (at + h), 1.0, 0.0) for h in (0, 8)], axis=0
        ).astype(BF16)

    loads[4].wait()
    image = jnp.dot(imgv[...].reshape(128, 768), order[...], preferred_element_type=F32)
    for ck in range(CH):
        xp[ck, :, 0:8, :] = zero_edge
        xp[ck, :, 24:32, :] = zero_edge
        gp[ck, :, 0:8, :] = zero_edge
        gp[ck, :, 24:32, :] = zero_edge
        xp[ck, :, 8:24, :] = image[:, ck * 128 : (ck + 1) * 128].reshape(8, 16, 128)
    K[...] = jnp.zeros_like(K)
    ZSf[...] = jnp.zeros_like(ZSf)
    loads[5].wait()

    @pl.when(source)
    def _():
        landed(zbuf.at[pl.ds(0, 3)], r_z)

    @pl.when(jnp.logical_not(source))
    def _():
        landed(zbuf, r_z)

    rows = lax.broadcasted_iota(jnp.int32, (48, 64), 0)
    cols = lax.broadcasted_iota(jnp.int32, (48, 64), 1)
    pick48 = jnp.where(rows // 12 * 16 + rows % 12 == cols, 1.0, 0.0).astype(BF16)
    packed = jnp.dot(pick48, zbuf[...].reshape(64, 896), preferred_element_type=F32)
    W[yl, x] = packed[:, :768].astype(BF16)
    slot = yl * QUAD + x
    S[slot] = (packed[0:24, 768:] + pltpu.roll(packed[24:48, 768:], 64, 1)).astype(BF16)

    for k in range(1, 16):
        rcopy(S.at[slot], S.at[slot], s_g2, r_g2, dxy(k // 4, dy_of(k % 4))).start()
    A, B = pl.ds(0, 384), pl.ds(384, 384)
    for i in range(1, 4):
        rcopy(W.at[yl, x, :, A], W.at[yl, x, :, A], s_w.at[0], r_w.at[0], dxy(0, dy_of(i))).start()
        rcopy(W.at[yl, x, :, B], W.at[yl, x, :, B], s_w.at[1], r_w.at[1], dxy(i, 0)).start()

    landed(W.at[0, pl.ds(0, 3), :, A], r_w.at[0])
    for i in range(1, 4):
        rcopy(W.at[:, x, :, A], W.at[:, x, :, A], s_w.at[2], r_w.at[2], dxy(i, 0)).start()
    landed(W.at[0, pl.ds(0, 3), :, B], r_w.at[1])
    for i in range(1, 4):
        rcopy(W.at[yl, :, :, B], W.at[yl, :, :, B], s_w.at[3], r_w.at[3], dxy(0, dy_of(i))).start()

    landed(S.at[pl.ds(0, 15)], r_g2)
    flat = S[...].astype(F32)
    other = pltpu.roll(flat.reshape(384, 128), 64, 1).reshape(16, 24, 128)
    kcols = jnp.transpose(jnp.concatenate([flat, other], axis=1).reshape(768, 128))
    for ck in range(CH):
        kT[ck] = kcols[:64, ck * 128 : (ck + 1) * 128]

    @pl.loop(0, CH)
    def _(ck):
        acc = [jnp.zeros((16, 128), F32) for _ in range(8)]
        for b in range(KS):
            taps = [kT[ck, pl.ds(a * KS + b, 1), :] for a in range(KS)]
            for row in range(8):
                xs = xp[ck, row, pl.ds(5 + b, 16), :]
                for a in range(KS):
                    h = row - a + 3
                    if 0 <= h < 8:
                        acc[h] = acc[h] + xs * taps[a]
        for h in range(8):
            cv[ck, h] = acc[h]

    @pl.loop(0, 8)
    def _(h):
        v = [cv[ck, h] for ck in range(CH)]
        total = v[0]
        for ck in range(1, CH):
            total = total + v[ck]
        avg = jnp.sum(total, axis=-1, keepdims=True) * (1.0 / 768)
        v = [u - avg for u in v]
        total = v[0] * v[0]
        for ck in range(1, CH):
            total = total + v[ck] * v[ck]
        inv = lax.rsqrt(jnp.sum(total, axis=-1, keepdims=True) * (1.0 / 768) + EPS)
        istd[h] = jnp.broadcast_to(inv, (16, 128))
        for ck in range(CH):
            w = v[ck] * inv
            cv[ck, h] = w
            N[core, pl.ds(pl.multiple_of(h * 16, 16), 16), ck * 128 : (ck + 1) * 128] = (
                w * kT[ck, 49:50, :] + kT[ck, 50:51, :]
            ).astype(BF16)

    n_send = rcopy(N.at[core], N.at[core], s_c.at[1], r_c.at[1], sib)
    n_send.start()

    def flip(c):
        NT[:, pl.ds(pl.multiple_of(c * 128, 128), 128)] = jnp.transpose(N[c].astype(F32)).astype(BF16)

    flip(core)
    n_send.wait_recv()
    flip(1 - core)
    cot_send.wait_recv()

    def pointwise(cols):
        pre[:, cols] = jnp.dot(
            N[...].reshape(256, 768), W[:, :, :, cols].reshape(768, 384), preferred_element_type=F32
        )

    landed(W.at[pl.ds(0, 3), :, :, A], r_w.at[2])
    pointwise(slice(0, 384))
    landed(W.at[pl.ds(0, 3), :, :, B], r_w.at[3])
    pointwise(slice(384, 768))

    @pl.loop(0, 8)
    def _(i):
        at = pl.ds(pl.multiple_of(i * 16, 16), 16)
        for c in range(2):
            slope = gelu_slope(pre[pl.ds(pl.multiple_of(c * 128 + i * 16, 16), 16), :])
            G[c, at, :] = (Ct[c, at, :].astype(F32) * slope).astype(BF16)

    xf = lax.rem(x + sgn + NX, NX)
    xb = lax.rem(x - sgn + NX, NX)
    to_f, to_b = dxy(sgn, 0), dxy(-sgn, 0)
    pieces = [(j, lax.rem(yl + j, NYL)) for j in (0, 1, 3, 2)]
    for j, q in pieces:
        part = jnp.dot(
            NT[pl.ds(pl.multiple_of(q * 192, 64), 192), :], G[...].reshape(256, 768),
            preferred_element_type=F32,
        ).reshape(QUAD, 48, 768)
        Pf[q] = part
        Pb[q] = part.astype(BF16)
        rcopy(Pb.at[q, lax.rem(x + 2, NX)], F.at[j], s_m.at[0], r_m1.at[j], to_f).start()
        rcopy(Pb.at[q, xb], RB.at[j], s_m.at[1], r_m2.at[j], to_b).start()

    GN[...] = lax.dot_general(
        G[...].reshape(256, 768), W[...].reshape(768, 768), (((1,), (1,)), ((), ())),
        preferred_element_type=F32,
    ).reshape(2, 128, 768)
    gn_send = rcopy(GN.at[1 - core], GNr, s_c.at[2], r_c.at[2], sib)
    gn_send.start()

    def forward_x(j, q):
        landed(F.at[j], r_m1.at[j])
        TB[j] = (F[j].astype(F32) + Pf[q, xf]).astype(BF16)
        rcopy(TB.at[j], RF.at[j], s_m.at[2], r_m3.at[j], to_f).start()

    def into_y(j, q):
        landed(RB.at[j], r_m2.at[j])
        landed(RF.at[j], r_m3.at[j])
        total = Pf[q, x] + RB[j].astype(F32) + RF[j].astype(F32)
        SXb[q] = total.astype(BF16)
        for d in (j, j + 4):
            if d:
                cols = pl.ds(pl.multiple_of(lax.div(lax.rem(y + d, NY), NYL) * 384, 128), 384)
                rcopy(SXb.at[q, :, cols], RY.at[d - 1], s_y, r_y, dxy(0, d)).start()
        if j == 0:
            SX[...] = total

    forward_x(*pieces[0])
    gn_send.wait_recv()

    def ln_back(h, carry):
        at = pl.ds(pl.multiple_of(h * 16, 16), 16)
        sums_g, sums_b = carry
        gn = [
            GN[core, at, ck * 128 : (ck + 1) * 128] + GNr[at, ck * 128 : (ck + 1) * 128]
            for ck in range(CH)
        ]
        wh = [cv[ck, h] for ck in range(CH)]
        sums_b = [a + g for a, g in zip(sums_b, gn)]
        sums_g = [a + g * w for a, g, w in zip(sums_g, gn, wh)]
        gw = [g * kT[ck, 49:50, :] for ck, g in enumerate(gn)]
        t1, t2 = gw[0], gw[0] * wh[0]
        for ck in range(1, CH):
            t1 = t1 + gw[ck]
            t2 = t2 + gw[ck] * wh[ck]
        m_1 = jnp.sum(t1, axis=-1, keepdims=True) * (1.0 / 768)
        m_2 = jnp.sum(t2, axis=-1, keepdims=True) * (1.0 / 768)
        inv = istd[h]
        for ck in range(CH):
            gp[ck, h, 8:24, :] = inv * (gw[ck] - m_1 - wh[ck] * m_2)
        return sums_g, sums_b

    zeros = [jnp.zeros((16, 128), F32) for _ in range(CH)]
    sums_g, sums_b = lax.fori_loop(0, 8, ln_back, (zeros, zeros))
    for ck in range(CH):
        K[ck, 49:50, :] = jnp.sum(sums_g[ck], axis=0, keepdims=True)
        K[ck, 50:51, :] = jnp.sum(sums_b[ck], axis=0, keepdims=True)
    forward_x(*pieces[1])

    def kernel_grad(ck):
        g = [gp[ck, h, 8:24, :] for h in range(8)]
        for b in range(KS):
            acc = [None] * KS
            for row in range(8):
                xs = xp[ck, row, pl.ds(5 + b, 16), :]
                for a in range(KS):
                    h = row - a + 3
                    if 0 <= h < 8:
                        t = xs * g[h]
                        acc[a] = t if acc[a] is None else acc[a] + t
            for a in range(KS):
                K[ck, a * KS + b : a * KS + b + 1, :] = jnp.sum(acc[a], axis=0, keepdims=True)

    pl.loop(0, CH // 2)(kernel_grad)
    forward_x(*pieces[2])
    pl.loop(CH // 2, CH)(kernel_grad)
    forward_x(*pieces[3])

    for ck in range(CH):
        Kt[ck * 128 : (ck + 1) * 128, :] = jnp.transpose(K[ck])
    kt = Kt[...].reshape(16, 48, 128)
    kt = kt[:, :24] + pltpu.roll(kt[:, 24:].reshape(384, 128), 64, 1).reshape(16, 24, 128)
    Kf[...] = kt
    Kb[...] = kt.astype(BF16)
    for k in range(1, 16):
        qx, ql = lax.rem(x + k // 4, NX), lax.rem(yl + dy_of(k % 4) + NYL, NYL)
        rcopy(Kb.at[ql * QUAD + qx], RK.at[k - 1], s_k, r_k, dxy(k // 4, dy_of(k % 4))).start()

    for piece in pieces:
        into_y(*piece)

    landed(RK, r_k)
    ksum = Kf[slot]
    for k in range(15):
        ksum = ksum + RK[k].astype(F32)
    KS_[0:24, :] = ksum
    KS_[24:48, :] = pltpu.roll(ksum, 64, 1)
    landed(RY, r_y)
    ysum = SX[:, pl.ds(pl.multiple_of(yh * 384, 128), 384)]
    for d in range(NY - 1):
        ysum = ysum + RY[d].astype(F32)
    SY[...] = ysum
    for j in range(QUAD):
        ZSf[j, 0:12, 0:384] = SY[12 * j : 12 * j + 12, :]
        ZSf[j, 0:12, 384:512] = KS_[12 * j : 12 * j + 12, :]
    ZS[...] = ZSf[...].astype(BF16)
    for j in range(QUAD):
        @pl.when(x + QUAD * j != z)
        def _():
            rcopy(ZS.at[j], RZ.at[z], s_z2, r_z2, dev(x, y, x + QUAD * j, core)).start()

    @pl.loop(0, CH)
    def _(ck):
        acc = [jnp.zeros((16, 128), F32) for _ in range(8)]
        for b in range(KS):
            taps = [kT[ck, pl.ds(a * KS + b, 1), :] for a in range(KS)]
            for row in range(8):
                gs = gp[ck, row, pl.ds(11 - b, 16), :]
                for a in range(KS):
                    h = row + a - 3
                    if 0 <= h < 8:
                        acc[h] = acc[h] + gs * taps[a]
        lanes = pl.ds(pl.multiple_of(ck * 128, 128), 128)
        for h in range(8):
            gip[h, :, lanes] = acc[h].astype(BF16)

    gi_ref[...] = lax.dot_general(
        gip[...].reshape(128, 768), order[...], (((1,), (1,)), ((), ())), preferred_element_type=F32
    ).reshape(8, 16, 768).astype(BF16)

    p = yh * NC + core

    @pl.when(source)
    def _():
        RZ[z] = ZS[zr]
        landed(RZ.at[pl.ds(0, 15)], r_z2)
        total = RZ[0].astype(F32)
        for k in range(1, NZ):
            total = total + RZ[k].astype(F32)
        FIN[...] = total
        for i in range(1, NX):
            rcopy(FIN, PC.at[p], s_r1, r_r1, dxy(i, 0)).start()
        PC[p] = total

    @pl.when(jnp.logical_not(source))
    def _():
        landed(FIN, r_r1)

    for to in (sib, dxy(0, NYL), far):
        rcopy(PC.at[p], PC.at[p], s_r2, r_r2, to).start()
    landed(PC.at[pl.ds(0, 3)], r_r2)
    for q in range(4):
        at = (q % NC) * 768 + (q // NC) * 384
        gu_ref[:, at : at + 384] = PC[q, 0:12, 0:384]
    sm_ref[...] = (PC[0, 0:12, 384:] + PC[1, 0:12, 384:]) + (PC[2, 0:12, 384:] + PC[3, 0:12, 384:])

    @pl.when(source)
    def _():
        left(zall, s_z)
        left(PC.at[pl.ds(0, 3)], s_r1)
        left(ZS.at[pl.ds(0, 3)], s_z2)

    @pl.when(jnp.logical_not(source))
    def _():
        left(ZS, s_z2)

    for c in (cot_send, n_send, gn_send):
        c.wait_send()
    left(S.at[pl.ds(0, 15)], s_g2)
    left(W.at[0, pl.ds(0, 3), :, A], s_w.at[0])
    left(W.at[0, pl.ds(0, 3), :, B], s_w.at[1])
    left(W.at[pl.ds(0, 3), :, :, A], s_w.at[2])
    left(W.at[pl.ds(0, 3), :, :, B], s_w.at[3])
    for i in range(3):
        left(TB, s_m.at[i])
    left(RY, s_y)
    left(RK, s_k)
    left(PC.at[pl.ds(0, 3)], s_r2)


def body(images, cotangent, depthwise_weight, norm_gain, norm_bias, up_weight):
    pixels = (
        images.shape[0] * images.shape[1] * images.shape[2]
        * lax.axis_size("shard") * lax.axis_size("rep")
    )
    factor = 1.0 / math.sqrt(pixels)
    dma = pltpu.SemaphoreType.DMA
    vm = lambda dtype, *shape: pltpu.VMEM(shape, dtype)
    gi, gu, sm = pl.pallas_call(
        kernel,
        out_shape=(
            jax.ShapeDtypeStruct((8, 16, 768), BF16),
            jax.ShapeDtypeStruct((12, 1536), F32),
            jax.ShapeDtypeStruct((12, 128), F32),
        ),
        in_specs=[pl.BlockSpec(memory_space=pltpu.HBM)] * 6,
        out_specs=[pl.BlockSpec(memory_space=pltpu.VMEM)] * 3,
        scratch_shapes=[
            vm(BF16, 8, 16, 768),
            vm(BF16, 768, 768),
            vm(BF16, 8, 16, 768),
            vm(BF16, 12, 1536),
            vm(BF16, 12, 49),
            vm(BF16, 1, 12),
            vm(BF16, 1, 12),
            vm(F32, 16, 896),
            vm(BF16, 16, 896),
            vm(BF16, 15, 16, 896),
            vm(BF16, 4, 16, 896),
            vm(BF16, 4, 4, 48, 768),
            vm(BF16, 16, 24, 128),
            vm(F32, CH, 64, 128),
            vm(F32, CH, 8, 32, 128),
            vm(F32, CH, 8, 32, 128),
            vm(F32, CH, 8, 16, 128),
            vm(F32, 8, 16, 128),
            vm(BF16, 2, 128, 768),
            vm(BF16, 768, 256),
            vm(BF16, 2, 128, 768),
            vm(F32, 256, 768),
            vm(BF16, 2, 128, 768),
            vm(F32, 2, 128, 768),
            vm(F32, 128, 768),
            vm(F32, 4, 4, 48, 768),
            vm(BF16, 4, 4, 48, 768),
            vm(BF16, 4, 48, 768),
            vm(BF16, 4, 48, 768),
            vm(BF16, 4, 48, 768),
            vm(BF16, 4, 48, 768),
            vm(F32, 48, 768),
            vm(BF16, 4, 48, 768),
            vm(BF16, 7, 48, 384),
            vm(F32, 48, 384),
            vm(F32, CH, 128, 128),
            vm(F32, 768, 128),
            vm(F32, 16, 24, 128),
            vm(BF16, 16, 24, 128),
            vm(BF16, 15, 24, 128),
            vm(F32, 48, 128),
            vm(F32, 4, 16, 512),
            vm(BF16, 4, 16, 512),
            vm(BF16, 16, 16, 512),
            vm(F32, 16, 512),
            vm(F32, 4, 16, 512),
            dma((6,)),
            dma, dma,
            dma, dma,
            dma((4,)), dma((4,)),
            dma((3,)), dma((3,)),
            dma((3,)), dma((4,)), dma((4,)), dma((4,)),
            dma, dma,
            dma, dma,
            dma, dma,
            dma, dma,
            dma, dma,
        ],
        compiler_params=pltpu.CompilerParams(
            collective_id=0, has_side_effects=True, vmem_limit_bytes=40 << 20
        ),
    )(
        *[
            pltpu.with_memory_space_constraint(v, pltpu.HBM)
            for v in (
                images.reshape(8, 16, 768), cotangent.reshape(128, 1536), depthwise_weight,
                norm_gain.reshape(1, 12), norm_bias.reshape(1, 12), up_weight,
            )
        ]
    )
    taps = KS * KS
    sm = sm * factor
    return (gi.reshape(images.shape), gu * factor, sm[:, :taps], sm[:, taps], sm[:, taps + 1])


def solution(mesh):
    placed = (
        P(("shard", "rep"), None, None, None),
        P(("shard", "rep"), None, None, None),
        P("shard", None),
        P("shard"),
        P("shard"),
        P("shard", None),
    )
    return jax.shard_map(
        body,
        mesh=mesh,
        in_specs=placed,
        out_specs=(
            P(("shard", "rep"), None, None, None),
            P("shard", None),
            P("shard", None),
            P("shard"),
            P("shard"),
        ),
        check_vma=False,
    )
```

```python
import math

import jax
import jax.numpy as jnp
from jax import lax
from jax.experimental import pallas as pl
from jax.experimental.pallas import tpu as pltpu
from jax.sharding import PartitionSpec as P

KS = 7
EPS = 1e-06
F32 = jnp.float32
BF16 = jnp.bfloat16
MESH = pl.DeviceIdType.MESH

NX, NYL, NYH, NZ, NC = 4, 4, 2, 16, 2
NY = NYL * NYH
QUAD = 4
CH = 6
FAR_FIRST = sorted(range(1, NZ), key=lambda k: abs(k - NZ // 2))


def gelu_slope(v):
    cumulative = 0.5 * (1.0 + lax.erf(v * 0.7071067811865476))
    return cumulative + v * jnp.exp(-0.5 * v * v) * 0.3989422804014327


def kernel(
    img_hbm, cot_hbm, dw_hbm, gain_hbm, bias_hbm, up_hbm,
    gi_ref, gu_ref, sm_ref,
    gip, order, imgv, upv, dwv, gnv, bsv, wlf, sml, wl, zall,
    zbuf, W, S, kT, xp, gp, cv, istd, N, NT, Ct, pre, G, GN, GNr,
    Pf, Pb, F, RB, RF, TB, SX, SXb, RY, SY, K, Kt, Kf, Kb, RK, KS_, ZSf, ZS, RZ, FIN, PH, PC,
    s_in, s_z, r_z, s_g2, r_g2, s_w, r_w, s_c, r_c,
    s_m, r_m1, r_m2, r_m3, s_y, r_y, s_k, r_k, s_z2, r_z2, s_r1, r_r1, s_r2, r_r2,
):
    s = lax.axis_index("shard")
    r = lax.axis_index("rep")
    yl, z = lax.div(s, NZ), lax.rem(s, NZ)
    x = lax.div(r, NYH * NC)
    yh = lax.rem(lax.div(r, NC), NYH)
    core = lax.rem(r, NC)
    y = yh * NYL + yl
    sgn = 1 - 2 * core
    zr = lax.div(z, QUAD)
    source = lax.rem(z, QUAD) == x

    def dev(x_, y_, z_, c_):
        return (
            lax.rem(y_, NYL) * NZ + z_,
            x_ * (NYH * NC) + lax.div(y_, NYL) * NC + c_,
        )

    def dz(k):
        return dev(x, y, lax.rem(z + k, NZ), core)

    def dxy(dx, dy):
        return dev(lax.rem(x + dx + 2 * NX, NX), lax.rem(y + dy + 2 * NY, NY), z, core)

    sib = dev(x, y, z, 1 - core)

    def rcopy(src, dst, ss, rs, to):
        return pltpu.make_async_remote_copy(
            src_ref=src, dst_ref=dst, send_sem=ss, recv_sem=rs, device_id=to, device_id_type=MESH
        )

    def landed(ref, sem):
        rcopy(ref, ref, s_in.at[0], sem, sib).wait_recv()

    def left(ref, sem):
        rcopy(ref, ref, sem, s_in.at[0], sib).wait_send()

    def dy_of(i):
        return (0, 1, -1, 2 * sgn)[i]

    half_own = pl.ds(pl.multiple_of(core * 768, 128), 768)
    half_sib = pl.ds(pl.multiple_of((1 - core) * 768, 128), 768)

    barrier = pltpu.get_barrier_semaphore()

    def hello(to):
        pl.semaphore_signal(barrier, inc=1, device_id=to, device_id_type=MESH)

    @pl.when(source)
    def _():
        for k in FAR_FIRST:
            hello(dz(k))

    @pl.when(jnp.logical_not(source))
    def _():
        for j in range(QUAD):
            hello(dev(x, y, x + QUAD * j, core))

    loads = [
        pltpu.make_async_copy(src, dst, s_in.at[i])
        for i, (src, dst) in enumerate(
            [(up_hbm, upv), (dw_hbm, dwv), (gain_hbm, gnv), (bias_hbm, bsv), (img_hbm, imgv),
             (cot_hbm.at[:, half_own], Ct.at[core])]
        )
    ]
    for c in loads:
        c.start()
    for d in range(1, NY):
        hello(dxy(0, d))
    for dx in range(1, NX):
        for i in range(4):
            hello(dxy(-dx, -dy_of(i)))
    hello(sib)
    for dy in (2, NY - 2):
        hello(dev(x, lax.rem(y + dy, NY), z, 1 - core))

    wlf[...] = jnp.zeros_like(wlf)
    for c in loads[:4]:
        c.wait()
    wlf[0:12, 0:768] = upv[:, half_own].astype(F32)
    sml[...] = jnp.zeros_like(sml)
    sml[:, 0:49] = dwv[...].astype(F32)
    row12 = lax.broadcasted_iota(jnp.int32, (12, 12), 0)
    col12 = lax.broadcasted_iota(jnp.int32, (12, 12), 1)

    def column(v):
        return jnp.sum(jnp.where(row12 == col12, v[...].astype(F32), 0.0), axis=1, keepdims=True)

    lane = lax.broadcasted_iota(jnp.int32, (12, 128), 1)
    extra = jnp.where(lane == 49, column(gnv), jnp.where(lane == 50, column(bsv), 0.0))
    sml[...] = sml[...] + extra
    for t in range(3):
        wlf[12:16, t * 128 : (t + 1) * 128] = sml[4 * t : 4 * t + 4, :]
    wl[...] = wlf[...].astype(BF16)
    pl.semaphore_wait(barrier, 26 + 11 * source.astype(jnp.int32))

    @pl.when(source)
    def _():
        for k in FAR_FIRST:
            rcopy(wl, zbuf.at[zr], s_z, r_z, dz(k)).start()

        zbuf[zr] = wl[...]

    cot_send = rcopy(cot_hbm.at[:, half_sib], Ct.at[core], s_c.at[0], r_c.at[0], sib)
    cot_send.start()

    zero_edge = jnp.zeros((8, 8, 128), F32)
    place = lax.broadcasted_iota(jnp.int32, (8, 768), 1)
    block, inner = place // 48, place % 48
    channel = (block // QUAD * NZ + block % QUAD + QUAD * (inner // 12)) * 12 + inner % 12
    near = lax.broadcasted_iota(jnp.int32, (8, 768), 0)

    @pl.loop(0, 48)
    def _(i):
        at = pl.multiple_of(i * 16, 16)
        order[pl.ds(at, 16), :] = jnp.concatenate(
            [jnp.where(channel == near + (at + h), 1.0, 0.0) for h in (0, 8)], axis=0
        ).astype(BF16)

    loads[4].wait()
    image = jnp.dot(imgv[...].reshape(128, 768), order[...], preferred_element_type=F32)
    for ck in range(CH):
        xp[ck, :, 0:8, :] = zero_edge
        xp[ck, :, 24:32, :] = zero_edge
        gp[ck, :, 0:8, :] = zero_edge
        gp[ck, :, 24:32, :] = zero_edge
        xp[ck, :, 8:24, :] = image[:, ck * 128 : (ck + 1) * 128].reshape(8, 16, 128)
    K[...] = jnp.zeros_like(K)
    loads[5].wait()

    @pl.when(source)
    def _():
        landed(zbuf.at[pl.ds(0, 3)], r_z)

    @pl.when(jnp.logical_not(source))
    def _():
        landed(zbuf, r_z)

    rows = lax.broadcasted_iota(jnp.int32, (48, 64), 0)
    cols = lax.broadcasted_iota(jnp.int32, (48, 64), 1)
    pick48 = jnp.where(rows // 12 * 16 + rows % 12 == cols, 1.0, 0.0).astype(BF16)
    blocks = zbuf[...].reshape(64, 768)
    W[yl, x] = jnp.dot(pick48, blocks, preferred_element_type=F32).astype(BF16)
    small = jnp.zeros((48, 128), F32)
    for t in range(3):
        here = jnp.logical_and(rows % 12 // 4 == t, rows // 12 * 16 + 12 + rows % 4 == cols)
        small = small + jnp.dot(
            jnp.where(here, 1.0, 0.0).astype(BF16), blocks[:, t * 128 : (t + 1) * 128],
            preferred_element_type=F32,
        )
    slot = yl * QUAD + x
    S[slot] = (small[0:24] + pltpu.roll(small[24:48], 64, 1)).astype(BF16)

    A, B = pl.ds(0, 384), pl.ds(384, 384)
    for i in range(1, 4):
        rcopy(W.at[yl, x, :, A], W.at[yl, x, :, A], s_w.at[0], r_w.at[0], dxy(0, dy_of(i))).start()
        rcopy(W.at[yl, x, :, B], W.at[yl, x, :, B], s_w.at[1], r_w.at[1], dxy(i, 0)).start()
    for k in range(1, 16):
        rcopy(S.at[slot], S.at[slot], s_g2, r_g2, dxy(k // 4, dy_of(k % 4))).start()

    landed(W.at[0, pl.ds(0, 3), :, A], r_w.at[0])
    for i in range(1, 4):
        rcopy(W.at[:, x, :, A], W.at[:, x, :, A], s_w.at[2], r_w.at[2], dxy(i, 0)).start()
    landed(W.at[0, pl.ds(0, 3), :, B], r_w.at[1])
    for i in range(1, 4):
        rcopy(W.at[yl, :, :, B], W.at[yl, :, :, B], s_w.at[3], r_w.at[3], dxy(0, dy_of(i))).start()

    landed(S.at[pl.ds(0, 15)], r_g2)
    flat = S[...].astype(F32)
    other = pltpu.roll(flat.reshape(384, 128), 64, 1).reshape(16, 24, 128)
    kcols = jnp.transpose(jnp.concatenate([flat, other], axis=1).reshape(768, 128))
    for ck in range(CH):
        kT[ck] = kcols[:64, ck * 128 : (ck + 1) * 128]

    @pl.loop(0, CH)
    def _(ck):
        acc = [jnp.zeros((16, 128), F32) for _ in range(8)]
        for b in range(KS):
            taps = [kT[ck, pl.ds(a * KS + b, 1), :] for a in range(KS)]
            for row in range(8):
                xs = xp[ck, row, pl.ds(5 + b, 16), :]
                for a in range(KS):
                    h = row - a + 3
                    if 0 <= h < 8:
                        acc[h] = acc[h] + xs * taps[a]
        for h in range(8):
            cv[ck, h] = acc[h]

    @pl.loop(0, 8)
    def _(h):
        v = [cv[ck, h] for ck in range(CH)]
        total = v[0]
        for ck in range(1, CH):
            total = total + v[ck]
        avg = jnp.sum(total, axis=-1, keepdims=True) * (1.0 / 768)
        v = [u - avg for u in v]
        total = v[0] * v[0]
        for ck in range(1, CH):
            total = total + v[ck] * v[ck]
        inv = lax.rsqrt(jnp.sum(total, axis=-1, keepdims=True) * (1.0 / 768) + EPS)
        istd[h] = jnp.broadcast_to(inv, (16, 128))
        for ck in range(CH):
            w = v[ck] * inv
            cv[ck, h] = w
            N[core, pl.ds(pl.multiple_of(h * 16, 16), 16), ck * 128 : (ck + 1) * 128] = (
                w * kT[ck, 49:50, :] + kT[ck, 50:51, :]
            ).astype(BF16)

    n_send = rcopy(N.at[core], N.at[core], s_c.at[1], r_c.at[1], sib)
    n_send.start()

    def flip(c):
        NT[:, pl.ds(pl.multiple_of(c * 128, 128), 128)] = jnp.transpose(N[c].astype(F32)).astype(BF16)

    flip(core)
    n_send.wait_recv()
    flip(1 - core)
    cot_send.wait_recv()

    def pointwise(cols):
        pre[:, cols] = jnp.dot(
            N[...].reshape(256, 768), W[:, :, :, cols].reshape(768, 384), preferred_element_type=F32
        )

    landed(W.at[pl.ds(0, 3), :, :, A], r_w.at[2])
    pointwise(slice(0, 384))
    landed(W.at[pl.ds(0, 3), :, :, B], r_w.at[3])
    pointwise(slice(384, 768))

    @pl.loop(0, 8)
    def _(i):
        at = pl.ds(pl.multiple_of(i * 16, 16), 16)
        for c in range(2):
            slope = gelu_slope(pre[pl.ds(pl.multiple_of(c * 128 + i * 16, 16), 16), :])
            G[c, at, :] = (Ct[c, at, :].astype(F32) * slope).astype(BF16)

    xf = lax.rem(x + sgn + NX, NX)
    xb = lax.rem(x - sgn + NX, NX)
    to_f, to_b = dxy(sgn, 0), dxy(-sgn, 0)
    pieces = [(j, lax.rem(yl + j, NYL)) for j in (2, 3, 1, 0)]
    for j, q in pieces:
        part = jnp.dot(
            NT[pl.ds(pl.multiple_of(q * 192, 64), 192), :], G[...].reshape(256, 768),
            preferred_element_type=F32,
        ).reshape(QUAD, 48, 768)
        Pf[q] = part
        Pb[q] = part.astype(BF16)
        rcopy(Pb.at[q, lax.rem(x + 2, NX)], F.at[j], s_m.at[0], r_m1.at[j], to_f).start()
        rcopy(Pb.at[q, xb], RB.at[j], s_m.at[1], r_m2.at[j], to_b).start()

    GN[...] = lax.dot_general(
        G[...].reshape(256, 768), W[...].reshape(768, 768), (((1,), (1,)), ((), ())),
        preferred_element_type=F32,
    ).reshape(2, 128, 768)
    gn_send = rcopy(GN.at[1 - core], GNr, s_c.at[2], r_c.at[2], sib)
    gn_send.start()

    def forward_x(j, q):
        landed(F.at[j], r_m1.at[j])
        TB[j] = (F[j].astype(F32) + Pf[q, xf]).astype(BF16)
        rcopy(TB.at[j], RF.at[j], s_m.at[2], r_m3.at[j], to_f).start()

    def into_y(j, q):
        landed(RB.at[j], r_m2.at[j])
        landed(RF.at[j], r_m3.at[j])
        total = Pf[q, x] + RB[j].astype(F32) + RF[j].astype(F32)
        SXb[q] = total.astype(BF16)
        for d in ((j + 2) % 4, (j + 2) % 4 + 4):
            if d:
                cols = pl.ds(pl.multiple_of(lax.div(lax.rem(y + d, NY), NYL) * 384, 128), 384)
                rcopy(SXb.at[q, :, cols], RY.at[d - 1], s_y, r_y, dxy(0, d)).start()
        if j == 2:
            SX[...] = total

    forward_x(*pieces[0])
    gn_send.wait_recv()

    def ln_back(h, carry):
        at = pl.ds(pl.multiple_of(h * 16, 16), 16)
        sums_g, sums_b = carry
        gn = [
            GN[core, at, ck * 128 : (ck + 1) * 128] + GNr[at, ck * 128 : (ck + 1) * 128]
            for ck in range(CH)
        ]
        wh = [cv[ck, h] for ck in range(CH)]
        sums_b = [a + g for a, g in zip(sums_b, gn)]
        sums_g = [a + g * w for a, g, w in zip(sums_g, gn, wh)]
        gw = [g * kT[ck, 49:50, :] for ck, g in enumerate(gn)]
        t1, t2 = gw[0], gw[0] * wh[0]
        for ck in range(1, CH):
            t1 = t1 + gw[ck]
            t2 = t2 + gw[ck] * wh[ck]
        m_1 = jnp.sum(t1, axis=-1, keepdims=True) * (1.0 / 768)
        m_2 = jnp.sum(t2, axis=-1, keepdims=True) * (1.0 / 768)
        inv = istd[h]
        for ck in range(CH):
            gp[ck, h, 8:24, :] = inv * (gw[ck] - m_1 - wh[ck] * m_2)
        return sums_g, sums_b

    zeros = [jnp.zeros((16, 128), F32) for _ in range(CH)]
    sums_g, sums_b = lax.fori_loop(0, 8, ln_back, (zeros, zeros))
    for ck in range(CH):
        K[ck, 49:50, :] = jnp.sum(sums_g[ck], axis=0, keepdims=True)
        K[ck, 50:51, :] = jnp.sum(sums_b[ck], axis=0, keepdims=True)
    forward_x(*pieces[1])

    def kernel_grad(ck):
        g = [gp[ck, h, 8:24, :] for h in range(8)]
        for b in range(KS):
            acc = [None] * KS
            for row in range(8):
                xs = xp[ck, row, pl.ds(5 + b, 16), :]
                for a in range(KS):
                    h = row - a + 3
                    if 0 <= h < 8:
                        t = xs * g[h]
                        acc[a] = t if acc[a] is None else acc[a] + t
            for a in range(KS):
                K[ck, a * KS + b : a * KS + b + 1, :] = jnp.sum(acc[a], axis=0, keepdims=True)

    pl.loop(0, CH // 2)(kernel_grad)
    forward_x(*pieces[2])
    pl.loop(CH // 2, CH)(kernel_grad)
    forward_x(*pieces[3])

    for ck in range(CH):
        Kt[ck * 128 : (ck + 1) * 128, :] = jnp.transpose(K[ck])
    kt = Kt[...].reshape(16, 48, 128)
    kt = kt[:, :24] + pltpu.roll(kt[:, 24:].reshape(384, 128), 64, 1).reshape(16, 24, 128)
    Kf[...] = kt
    Kb[...] = kt.astype(BF16)
    for k in range(1, 16):
        qx, ql = lax.rem(x + k // 4, NX), lax.rem(yl + dy_of(k % 4) + 2 + NYL, NYL)
        rcopy(Kb.at[ql * QUAD + qx], RK.at[k - 1], s_k, r_k, dxy(k // 4, dy_of(k % 4))).start()

    for piece in pieces:
        into_y(*piece)

    landed(RK, r_k)
    ksum = Kf[lax.rem(yl + 2, NYL) * QUAD + x]
    for k in range(15):
        ksum = ksum + RK[k].astype(F32)
    KS_[0:24, :] = ksum
    KS_[24:48, :] = pltpu.roll(ksum, 64, 1)
    landed(RY, r_y)
    ysum = SX[:, pl.ds(pl.multiple_of(yh * 384, 128), 384)]
    for d in range(NY - 1):
        ysum = ysum + RY[d].astype(F32)
    SY[...] = ysum
    for j in range(QUAD):
        ZSf[j, 0:12, :] = SY[12 * j : 12 * j + 12, :]
        for t in range(3):
            ZSf[j, 12:16, t * 128 : (t + 1) * 128] = KS_[12 * j + 4 * t : 12 * j + 4 * t + 4, :]
    ZS[...] = ZSf[...].astype(BF16)
    for j in range(QUAD):
        @pl.when(x + QUAD * j != z)
        def _():
            rcopy(ZS.at[j], RZ.at[z], s_z2, r_z2, dev(x, y, x + QUAD * j, core)).start()

    @pl.loop(0, CH)
    def _(ck):
        acc = [jnp.zeros((16, 128), F32) for _ in range(8)]
        for b in range(KS):
            taps = [kT[ck, pl.ds(a * KS + b, 1), :] for a in range(KS)]
            for row in range(8):
                gs = gp[ck, row, pl.ds(11 - b, 16), :]
                for a in range(KS):
                    h = row + a - 3
                    if 0 <= h < 8:
                        acc[h] = acc[h] + gs * taps[a]
        lanes = pl.ds(pl.multiple_of(ck * 128, 128), 128)
        for h in range(8):
            gip[h, :, lanes] = acc[h].astype(BF16)

    gi_ref[...] = lax.dot_general(
        gip[...].reshape(128, 768), order[...], (((1,), (1,)), ((), ())), preferred_element_type=F32
    ).reshape(8, 16, 768).astype(BF16)

    p = yh * NC + core

    @pl.when(source)
    def _():
        RZ[z] = ZS[zr]
        landed(RZ.at[pl.ds(0, 15)], r_z2)
        total = RZ[0].astype(F32)
        for k in range(1, NZ):
            total = total + RZ[k].astype(F32)
        FIN[...] = total.astype(BF16)
        for i in range(1, NX):
            rcopy(FIN, PH, s_r1, r_r1, dxy(i, 0)).start()
        PH[...] = total.astype(BF16)

    @pl.when(jnp.logical_not(source))
    def _():
        landed(FIN, r_r1)

    for dy in (2, NY - 2):
        for c in (core, 1 - core):
            rcopy(PH, PC.at[p], s_r2, r_r2, dev(x, lax.rem(y + dy, NY), z, c)).start()
    landed(PC, r_r2)
    for q in range(4):
        at = (q % NC) * 768 + (q // NC) * 384
        gu_ref[:, at : at + 384] = PC[q].astype(F32)[0:12]
    spare = PC[0].astype(F32)[8:16]
    for q in range(1, 4):
        spare = spare + PC[q].astype(F32)[8:16]
    for t in range(3):
        sm_ref[4 * t : 4 * t + 4, :] = spare[4:8, t * 128 : (t + 1) * 128]

    @pl.when(source)
    def _():
        left(zall, s_z)
        left(PC.at[pl.ds(0, 3)], s_r1)
        left(ZS.at[pl.ds(0, 3)], s_z2)

    @pl.when(jnp.logical_not(source))
    def _():
        left(ZS, s_z2)

    for c in (cot_send, n_send, gn_send):
        c.wait_send()
    left(S.at[pl.ds(0, 15)], s_g2)
    left(W.at[0, pl.ds(0, 3), :, A], s_w.at[0])
    left(W.at[0, pl.ds(0, 3), :, B], s_w.at[1])
    left(W.at[pl.ds(0, 3), :, :, A], s_w.at[2])
    left(W.at[pl.ds(0, 3), :, :, B], s_w.at[3])
    for i in range(3):
        left(TB, s_m.at[i])
    left(RY, s_y)
    left(RK, s_k)
    left(PC, s_r2)


def body(images, cotangent, depthwise_weight, norm_gain, norm_bias, up_weight):
    pixels = (
        images.shape[0] * images.shape[1] * images.shape[2]
        * lax.axis_size("shard") * lax.axis_size("rep")
    )
    factor = 1.0 / math.sqrt(pixels)
    dma = pltpu.SemaphoreType.DMA
    vm = lambda dtype, *shape: pltpu.VMEM(shape, dtype)
    gi, gu, sm = pl.pallas_call(
        kernel,
        out_shape=(
            jax.ShapeDtypeStruct((8, 16, 768), BF16),
            jax.ShapeDtypeStruct((12, 1536), F32),
            jax.ShapeDtypeStruct((12, 128), F32),
        ),
        in_specs=[pl.BlockSpec(memory_space=pltpu.HBM)] * 6,
        out_specs=[pl.BlockSpec(memory_space=pltpu.VMEM)] * 3,
        scratch_shapes=[
            vm(BF16, 8, 16, 768),
            vm(BF16, 768, 768),
            vm(BF16, 8, 16, 768),
            vm(BF16, 12, 1536),
            vm(BF16, 12, 49),
            vm(BF16, 1, 12),
            vm(BF16, 1, 12),
            vm(F32, 16, 768),
            vm(F32, 12, 128),
            vm(BF16, 16, 768),
            vm(BF16, 15, 16, 768),
            vm(BF16, 4, 16, 768),
            vm(BF16, 4, 4, 48, 768),
            vm(BF16, 16, 24, 128),
            vm(F32, CH, 64, 128),
            vm(F32, CH, 8, 32, 128),
            vm(F32, CH, 8, 32, 128),
            vm(F32, CH, 8, 16, 128),
            vm(F32, 8, 16, 128),
            vm(BF16, 2, 128, 768),
            vm(BF16, 768, 256),
            vm(BF16, 2, 128, 768),
            vm(F32, 256, 768),
            vm(BF16, 2, 128, 768),
            vm(F32, 2, 128, 768),
            vm(F32, 128, 768),
            vm(F32, 4, 4, 48, 768),
            vm(BF16, 4, 4, 48, 768),
            vm(BF16, 4, 48, 768),
            vm(BF16, 4, 48, 768),
            vm(BF16, 4, 48, 768),
            vm(BF16, 4, 48, 768),
            vm(F32, 48, 768),
            vm(BF16, 4, 48, 768),
            vm(BF16, 7, 48, 384),
            vm(F32, 48, 384),
            vm(F32, CH, 128, 128),
            vm(F32, 768, 128),
            vm(F32, 16, 24, 128),
            vm(BF16, 16, 24, 128),
            vm(BF16, 15, 24, 128),
            vm(F32, 48, 128),
            vm(F32, 4, 16, 384),
            vm(BF16, 4, 16, 384),
            vm(BF16, 16, 16, 384),
            vm(BF16, 16, 384),
            vm(BF16, 16, 384),
            vm(BF16, 4, 16, 384),
            dma((6,)),
            dma, dma,
            dma, dma,
            dma((4,)), dma((4,)),
            dma((3,)), dma((3,)),
            dma((3,)), dma((4,)), dma((4,)), dma((4,)),
            dma, dma,
            dma, dma,
            dma, dma,
            dma, dma,
            dma, dma,
        ],
        compiler_params=pltpu.CompilerParams(
            collective_id=0, has_side_effects=True, vmem_limit_bytes=40 << 20
        ),
    )(
        *[
            pltpu.with_memory_space_constraint(v, pltpu.HBM)
            for v in (
                images.reshape(8, 16, 768), cotangent.reshape(128, 1536), depthwise_weight,
                norm_gain.reshape(1, 12), norm_bias.reshape(1, 12), up_weight,
            )
        ]
    )
    taps = KS * KS
    sm = sm * factor
    return (gi.reshape(images.shape), gu * factor, sm[:, :taps], sm[:, taps], sm[:, taps + 1])


def solution(mesh):
    placed = (
        P(("shard", "rep"), None, None, None),
        P(("shard", "rep"), None, None, None),
        P("shard", None),
        P("shard"),
        P("shard"),
        P("shard", None),
    )
    return jax.shard_map(
        body,
        mesh=mesh,
        in_specs=placed,
        out_specs=(
            P(("shard", "rep"), None, None, None),
            P("shard", None),
            P("shard", None),
            P("shard"),
            P("shard"),
        ),
        check_vma=False,
    )
```

```python
import functools
import math

import jax
import jax.numpy as jnp
from jax import lax
from jax.experimental import pallas as pl
from jax.experimental.pallas import tpu as pltpu
from jax.sharding import PartitionSpec as P

KS = 7
EPS = 1e-06
F32 = jnp.float32
BF16 = jnp.bfloat16
MESH = pl.DeviceIdType.MESH

NX, NYL, NYH, NZ, NC = 4, 4, 2, 16, 2
NY = NYL * NYH
QUAD = 4
CH = 6
FAR_FIRST = sorted(range(1, NZ), key=lambda k: abs(k - NZ // 2))


def gelu_slope(v):
    cumulative = 0.5 * (1.0 + lax.erf(v * 0.7071067811865476))
    return cumulative + v * jnp.exp(-0.5 * v * v) * 0.3989422804014327


def hand_over(*refs):
    n = len(refs) // 2
    copies = [pltpu.make_async_copy(refs[i], refs[n + i], refs[-1].at[i]) for i in range(n)]
    for c in copies:
        c.start()
    for c in copies:
        c.wait()


def kernel(
    factor,
    img_hbm, cot_hbm, dw_hbm, gain_hbm, bias_hbm, up_hbm,
    gi_ref, gu_ref, gd_ref, gg_ref, gb_ref,
    gip, order, imgv, upv, dwv, gnv, bsv, wlf, sml, wl, zall,
    zbuf, W, S, kT, xp, gp, cv, istd, N, NT, Ct, pre, G, GN, GNr,
    Pf, Pb, F, RB, RF, TB, SX, SXb, RY, SY, K, Kt, Kf, Kb, RK, KS_, ZSf, ZS, RZ, FIN, PH, PC,
    s_in, s_z, r_z, s_g2, r_g2, s_w, r_w, s_c, r_c,
    s_m, r_m1, r_m2, r_m3, s_y, r_y, s_k, r_k, s_z2, r_z2, s_r1, r_r1, s_r2, r_r2,
):
    s = lax.axis_index("shard")
    r = lax.axis_index("rep")
    yl, z = lax.div(s, NZ), lax.rem(s, NZ)
    x = lax.div(r, NYH * NC)
    yh = lax.rem(lax.div(r, NC), NYH)
    core = lax.rem(r, NC)
    y = yh * NYL + yl
    sgn = 1 - 2 * core
    zr = lax.div(z, QUAD)
    source = lax.rem(z, QUAD) == x

    def dev(x_, y_, z_, c_):
        return (
            lax.rem(y_, NYL) * NZ + z_,
            x_ * (NYH * NC) + lax.div(y_, NYL) * NC + c_,
        )

    def dz(k):
        return dev(x, y, lax.rem(z + k, NZ), core)

    def dxy(dx, dy):
        return dev(lax.rem(x + dx + 2 * NX, NX), lax.rem(y + dy + 2 * NY, NY), z, core)

    sib = dev(x, y, z, 1 - core)

    def rcopy(src, dst, ss, rs, to):
        return pltpu.make_async_remote_copy(
            src_ref=src, dst_ref=dst, send_sem=ss, recv_sem=rs, device_id=to, device_id_type=MESH
        )

    def landed(ref, sem):
        rcopy(ref, ref, s_in.at[0], sem, sib).wait_recv()

    def left(ref, sem):
        rcopy(ref, ref, sem, s_in.at[0], sib).wait_send()

    def dy_of(i):
        return (0, 1, -1, 2 * sgn)[i]

    half_own = pl.ds(pl.multiple_of(core * 768, 128), 768)
    half_sib = pl.ds(pl.multiple_of((1 - core) * 768, 128), 768)

    barrier = pltpu.get_barrier_semaphore()

    def hello(to):
        pl.semaphore_signal(barrier, inc=1, device_id=to, device_id_type=MESH)

    @pl.when(source)
    def _():
        for k in FAR_FIRST:
            hello(dz(k))

    @pl.when(jnp.logical_not(source))
    def _():
        for j in range(QUAD):
            hello(dev(x, y, x + QUAD * j, core))

    loads = [
        pltpu.make_async_copy(src, dst, s_in.at[i])
        for i, (src, dst) in enumerate(
            [(up_hbm, upv), (dw_hbm, dwv), (gain_hbm, gnv), (bias_hbm, bsv), (img_hbm, imgv),
             (cot_hbm.at[:, half_own], Ct.at[core])]
        )
    ]
    for c in loads:
        c.start()
    for d in range(1, NY):
        hello(dxy(0, d))
    for dx in range(1, NX):
        for i in range(4):
            hello(dxy(-dx, -dy_of(i)))
    hello(sib)
    for dy in (2, NY - 2):
        hello(dev(x, lax.rem(y + dy, NY), z, 1 - core))

    wlf[...] = jnp.zeros_like(wlf)
    for c in loads[:4]:
        c.wait()
    wlf[0:12, 0:768] = upv[:, half_own].astype(F32)
    sml[...] = jnp.zeros_like(sml)
    sml[:, 0:49] = dwv[...].astype(F32)
    row12 = lax.broadcasted_iota(jnp.int32, (12, 12), 0)
    col12 = lax.broadcasted_iota(jnp.int32, (12, 12), 1)

    def column(v):
        return jnp.sum(jnp.where(row12 == col12, v[...].astype(F32), 0.0), axis=1, keepdims=True)

    lane = lax.broadcasted_iota(jnp.int32, (12, 128), 1)
    extra = jnp.where(lane == 49, column(gnv), jnp.where(lane == 50, column(bsv), 0.0))
    sml[...] = sml[...] + extra
    for t in range(3):
        wlf[12:16, t * 128 : (t + 1) * 128] = sml[4 * t : 4 * t + 4, :]
    wl[...] = wlf[...].astype(BF16)
    pl.semaphore_wait(barrier, 26 + 11 * source.astype(jnp.int32))

    @pl.when(source)
    def _():
        for k in FAR_FIRST:
            rcopy(wl, zbuf.at[zr], s_z, r_z, dz(k)).start()

        zbuf[zr] = wl[...]

    cot_send = rcopy(cot_hbm.at[:, half_sib], Ct.at[core], s_c.at[0], r_c.at[0], sib)
    cot_send.start()

    zero_edge = jnp.zeros((8, 8, 128), F32)
    place = lax.broadcasted_iota(jnp.int32, (8, 768), 1)
    block, inner = place // 48, place % 48
    channel = (block // QUAD * NZ + block % QUAD + QUAD * (inner // 12)) * 12 + inner % 12
    near = lax.broadcasted_iota(jnp.int32, (8, 768), 0)

    @pl.loop(0, 48)
    def _(i):
        at = pl.multiple_of(i * 16, 16)
        order[pl.ds(at, 16), :] = jnp.concatenate(
            [jnp.where(channel == near + (at + h), 1.0, 0.0) for h in (0, 8)], axis=0
        ).astype(BF16)

    loads[4].wait()
    image = jnp.dot(imgv[...].reshape(128, 768), order[...], preferred_element_type=F32)
    for ck in range(CH):
        xp[ck, :, 0:8, :] = zero_edge
        xp[ck, :, 24:32, :] = zero_edge
        gp[ck, :, 0:8, :] = zero_edge
        gp[ck, :, 24:32, :] = zero_edge
        xp[ck, :, 8:24, :] = image[:, ck * 128 : (ck + 1) * 128].reshape(8, 16, 128)
    K[...] = jnp.zeros_like(K)
    loads[5].wait()

    @pl.when(source)
    def _():
        landed(zbuf.at[pl.ds(0, 3)], r_z)

    @pl.when(jnp.logical_not(source))
    def _():
        landed(zbuf, r_z)

    rows = lax.broadcasted_iota(jnp.int32, (48, 64), 0)
    cols = lax.broadcasted_iota(jnp.int32, (48, 64), 1)
    pick48 = jnp.where(rows // 12 * 16 + rows % 12 == cols, 1.0, 0.0).astype(BF16)
    blocks = zbuf[...].reshape(64, 768)
    W[yl, x] = jnp.dot(pick48, blocks, preferred_element_type=F32).astype(BF16)
    small = jnp.zeros((48, 128), F32)
    for t in range(3):
        here = jnp.logical_and(rows % 12 // 4 == t, rows // 12 * 16 + 12 + rows % 4 == cols)
        small = small + jnp.dot(
            jnp.where(here, 1.0, 0.0).astype(BF16), blocks[:, t * 128 : (t + 1) * 128],
            preferred_element_type=F32,
        )
    slot = yl * QUAD + x
    S[slot] = (small[0:24] + pltpu.roll(small[24:48], 64, 1)).astype(BF16)

    A, B = pl.ds(0, 384), pl.ds(384, 384)
    for i in range(1, 4):
        rcopy(W.at[yl, x, :, A], W.at[yl, x, :, A], s_w.at[0], r_w.at[0], dxy(0, dy_of(i))).start()
        rcopy(W.at[yl, x, :, B], W.at[yl, x, :, B], s_w.at[1], r_w.at[1], dxy(i, 0)).start()
    for k in range(1, 16):
        rcopy(S.at[slot], S.at[slot], s_g2, r_g2, dxy(k // 4, dy_of(k % 4))).start()

    landed(W.at[0, pl.ds(0, 3), :, A], r_w.at[0])
    for i in range(1, 4):
        rcopy(W.at[:, x, :, A], W.at[:, x, :, A], s_w.at[2], r_w.at[2], dxy(i, 0)).start()
    landed(W.at[0, pl.ds(0, 3), :, B], r_w.at[1])
    for i in range(1, 4):
        rcopy(W.at[yl, :, :, B], W.at[yl, :, :, B], s_w.at[3], r_w.at[3], dxy(0, dy_of(i))).start()

    landed(S.at[pl.ds(0, 15)], r_g2)
    flat = S[...].astype(F32)
    other = pltpu.roll(flat.reshape(384, 128), 64, 1).reshape(16, 24, 128)
    kcols = jnp.transpose(jnp.concatenate([flat, other], axis=1).reshape(768, 128))
    for ck in range(CH):
        kT[ck] = kcols[:64, ck * 128 : (ck + 1) * 128]

    @pl.loop(0, CH)
    def _(ck):
        acc = [jnp.zeros((16, 128), F32) for _ in range(8)]
        for b in range(KS):
            taps = [kT[ck, pl.ds(a * KS + b, 1), :] for a in range(KS)]
            for row in range(8):
                xs = xp[ck, row, pl.ds(5 + b, 16), :]
                for a in range(KS):
                    h = row - a + 3
                    if 0 <= h < 8:
                        acc[h] = acc[h] + xs * taps[a]
        for h in range(8):
            cv[ck, h] = acc[h]

    @pl.loop(0, 8)
    def _(h):
        v = [cv[ck, h] for ck in range(CH)]
        total = v[0]
        for ck in range(1, CH):
            total = total + v[ck]
        avg = jnp.sum(total, axis=-1, keepdims=True) * (1.0 / 768)
        v = [u - avg for u in v]
        total = v[0] * v[0]
        for ck in range(1, CH):
            total = total + v[ck] * v[ck]
        inv = lax.rsqrt(jnp.sum(total, axis=-1, keepdims=True) * (1.0 / 768) + EPS)
        istd[h] = jnp.broadcast_to(inv, (16, 128))
        for ck in range(CH):
            w = v[ck] * inv
            cv[ck, h] = w
            N[core, pl.ds(pl.multiple_of(h * 16, 16), 16), ck * 128 : (ck + 1) * 128] = (
                w * kT[ck, 49:50, :] + kT[ck, 50:51, :]
            ).astype(BF16)

    n_send = rcopy(N.at[core], N.at[core], s_c.at[1], r_c.at[1], sib)
    n_send.start()

    def flip(c):
        NT[:, pl.ds(pl.multiple_of(c * 128, 128), 128)] = jnp.transpose(N[c].astype(F32)).astype(BF16)

    flip(core)
    n_send.wait_recv()
    flip(1 - core)
    cot_send.wait_recv()

    def pointwise(cols):
        pre[:, cols] = jnp.dot(
            N[...].reshape(256, 768), W[:, :, :, cols].reshape(768, 384), preferred_element_type=F32
        )

    landed(W.at[pl.ds(0, 3), :, :, A], r_w.at[2])
    pointwise(slice(0, 384))
    landed(W.at[pl.ds(0, 3), :, :, B], r_w.at[3])
    pointwise(slice(384, 768))

    @pl.loop(0, 8)
    def _(i):
        at = pl.ds(pl.multiple_of(i * 16, 16), 16)
        for c in range(2):
            slope = gelu_slope(pre[pl.ds(pl.multiple_of(c * 128 + i * 16, 16), 16), :])
            G[c, at, :] = (Ct[c, at, :].astype(F32) * slope).astype(BF16)

    xf = lax.rem(x + sgn + NX, NX)
    xb = lax.rem(x - sgn + NX, NX)
    to_f, to_b = dxy(sgn, 0), dxy(-sgn, 0)
    pieces = [(j, lax.rem(yl + j, NYL)) for j in (2, 3, 1, 0)]
    for j, q in pieces:
        part = jnp.dot(
            NT[pl.ds(pl.multiple_of(q * 192, 64), 192), :], G[...].reshape(256, 768),
            preferred_element_type=F32,
        ).reshape(QUAD, 48, 768)
        Pf[q] = part
        Pb[q] = part.astype(BF16)
        rcopy(Pb.at[q, lax.rem(x + 2, NX)], F.at[j], s_m.at[0], r_m1.at[j], to_f).start()
        rcopy(Pb.at[q, xb], RB.at[j], s_m.at[1], r_m2.at[j], to_b).start()

    GN[...] = lax.dot_general(
        G[...].reshape(256, 768), W[...].reshape(768, 768), (((1,), (1,)), ((), ())),
        preferred_element_type=F32,
    ).reshape(2, 128, 768)
    gn_send = rcopy(GN.at[1 - core], GNr, s_c.at[2], r_c.at[2], sib)
    gn_send.start()

    def forward_x(j, q):
        landed(F.at[j], r_m1.at[j])
        TB[j] = (F[j].astype(F32) + Pf[q, xf]).astype(BF16)
        rcopy(TB.at[j], RF.at[j], s_m.at[2], r_m3.at[j], to_f).start()

    def into_y(j, q):
        landed(RB.at[j], r_m2.at[j])
        landed(RF.at[j], r_m3.at[j])
        total = Pf[q, x] + RB[j].astype(F32) + RF[j].astype(F32)
        SXb[q] = total.astype(BF16)
        for d in ((j + 2) % 4, (j + 2) % 4 + 4):
            if d:
                cols = pl.ds(pl.multiple_of(lax.div(lax.rem(y + d, NY), NYL) * 384, 128), 384)
                rcopy(SXb.at[q, :, cols], RY.at[d - 1], s_y, r_y, dxy(0, d)).start()
        if j == 2:
            SX[...] = total

    forward_x(*pieces[0])
    gn_send.wait_recv()

    def ln_back(h, carry):
        at = pl.ds(pl.multiple_of(h * 16, 16), 16)
        sums_g, sums_b = carry
        gn = [
            GN[core, at, ck * 128 : (ck + 1) * 128] + GNr[at, ck * 128 : (ck + 1) * 128]
            for ck in range(CH)
        ]
        wh = [cv[ck, h] for ck in range(CH)]
        sums_b = [a + g for a, g in zip(sums_b, gn)]
        sums_g = [a + g * w for a, g, w in zip(sums_g, gn, wh)]
        gw = [g * kT[ck, 49:50, :] for ck, g in enumerate(gn)]
        t1, t2 = gw[0], gw[0] * wh[0]
        for ck in range(1, CH):
            t1 = t1 + gw[ck]
            t2 = t2 + gw[ck] * wh[ck]
        m_1 = jnp.sum(t1, axis=-1, keepdims=True) * (1.0 / 768)
        m_2 = jnp.sum(t2, axis=-1, keepdims=True) * (1.0 / 768)
        inv = istd[h]
        for ck in range(CH):
            gp[ck, h, 8:24, :] = inv * (gw[ck] - m_1 - wh[ck] * m_2)
        return sums_g, sums_b

    zeros = [jnp.zeros((16, 128), F32) for _ in range(CH)]
    sums_g, sums_b = lax.fori_loop(0, 8, ln_back, (zeros, zeros))
    for ck in range(CH):
        K[ck, 49:50, :] = jnp.sum(sums_g[ck], axis=0, keepdims=True)
        K[ck, 50:51, :] = jnp.sum(sums_b[ck], axis=0, keepdims=True)
    forward_x(*pieces[1])

    def kernel_grad(ck):
        g = [gp[ck, h, 8:24, :] for h in range(8)]
        for b in range(KS):
            acc = [None] * KS
            for row in range(8):
                xs = xp[ck, row, pl.ds(5 + b, 16), :]
                for a in range(KS):
                    h = row - a + 3
                    if 0 <= h < 8:
                        t = xs * g[h]
                        acc[a] = t if acc[a] is None else acc[a] + t
            for a in range(KS):
                K[ck, a * KS + b : a * KS + b + 1, :] = jnp.sum(acc[a], axis=0, keepdims=True)

    pl.loop(0, CH // 2)(kernel_grad)
    forward_x(*pieces[2])
    pl.loop(CH // 2, CH)(kernel_grad)
    forward_x(*pieces[3])

    for ck in range(CH):
        Kt[ck * 128 : (ck + 1) * 128, :] = jnp.transpose(K[ck])
    kt = Kt[...].reshape(16, 48, 128)
    kt = kt[:, :24] + pltpu.roll(kt[:, 24:].reshape(384, 128), 64, 1).reshape(16, 24, 128)
    Kf[...] = kt
    Kb[...] = kt.astype(BF16)
    for k in range(1, 16):
        qx, ql = lax.rem(x + k // 4, NX), lax.rem(yl + dy_of(k % 4) + 2 + NYL, NYL)
        rcopy(Kb.at[ql * QUAD + qx], RK.at[k - 1], s_k, r_k, dxy(k // 4, dy_of(k % 4))).start()

    for piece in pieces:
        into_y(*piece)

    landed(RK, r_k)
    ksum = Kf[lax.rem(yl + 2, NYL) * QUAD + x]
    for k in range(15):
        ksum = ksum + RK[k].astype(F32)
    KS_[0:24, :] = ksum
    KS_[24:48, :] = pltpu.roll(ksum, 64, 1)
    landed(RY, r_y)
    ysum = SX[:, pl.ds(pl.multiple_of(yh * 384, 128), 384)]
    for d in range(NY - 1):
        ysum = ysum + RY[d].astype(F32)
    SY[...] = ysum
    for j in range(QUAD):
        ZSf[j, 0:12, :] = SY[12 * j : 12 * j + 12, :]
        for t in range(3):
            ZSf[j, 12:16, t * 128 : (t + 1) * 128] = KS_[12 * j + 4 * t : 12 * j + 4 * t + 4, :]
    ZS[...] = ZSf[...].astype(BF16)
    for j in range(QUAD):
        @pl.when(x + QUAD * j != z)
        def _():
            rcopy(ZS.at[j], RZ.at[z], s_z2, r_z2, dev(x, y, x + QUAD * j, core)).start()

    @pl.loop(0, CH)
    def _(ck):
        acc = [jnp.zeros((16, 128), F32) for _ in range(8)]
        for b in range(KS):
            taps = [kT[ck, pl.ds(a * KS + b, 1), :] for a in range(KS)]
            for row in range(8):
                gs = gp[ck, row, pl.ds(11 - b, 16), :]
                for a in range(KS):
                    h = row + a - 3
                    if 0 <= h < 8:
                        acc[h] = acc[h] + gs * taps[a]
        lanes = pl.ds(pl.multiple_of(ck * 128, 128), 128)
        for h in range(8):
            gip[h, :, lanes] = acc[h].astype(BF16)

    gi_ref[...] = lax.dot_general(
        gip[...].reshape(128, 768), order[...], (((1,), (1,)), ((), ())), preferred_element_type=F32
    ).reshape(8, 16, 768).astype(BF16)

    p = yh * NC + core

    @pl.when(source)
    def _():
        RZ[z] = ZS[zr]
        landed(RZ.at[pl.ds(0, 15)], r_z2)
        total = RZ[0].astype(F32)
        for k in range(1, NZ):
            total = total + RZ[k].astype(F32)
        FIN[...] = total.astype(BF16)
        for i in range(1, NX):
            rcopy(FIN, PH, s_r1, r_r1, dxy(i, 0)).start()
        PH[...] = total.astype(BF16)

    @pl.when(jnp.logical_not(source))
    def _():
        landed(FIN, r_r1)

    for dy in (2, NY - 2):
        for c in (core, 1 - core):
            rcopy(PH, PC.at[p], s_r2, r_r2, dev(x, lax.rem(y + dy, NY), z, c)).start()
    landed(PC, r_r2)
    for q in range(4):
        at = (q % NC) * 768 + (q // NC) * 384
        gu_ref[:, at : at + 384] = PC[q].astype(F32)[0:12] * factor
    spare = PC[0].astype(F32)[8:16]
    for q in range(1, 4):
        spare = spare + PC[q].astype(F32)[8:16]
    for t in range(3):
        sml[4 * t : 4 * t + 4, :] = spare[4:8, t * 128 : (t + 1) * 128] * factor
    gd_ref[...] = sml[:, 0:49]

    def across(t):
        picked = jnp.sum(jnp.where(lane == t, sml[...], 0.0), axis=1, keepdims=True)
        return jnp.sum(jnp.where(row12 == col12, picked, 0.0), axis=0, keepdims=True)

    gg_ref[...] = across(49)
    gb_ref[...] = across(50)

    @pl.when(source)
    def _():
        left(zall, s_z)
        left(PC.at[pl.ds(0, 3)], s_r1)
        left(ZS.at[pl.ds(0, 3)], s_z2)

    @pl.when(jnp.logical_not(source))
    def _():
        left(ZS, s_z2)

    for c in (cot_send, n_send, gn_send):
        c.wait_send()
    left(S.at[pl.ds(0, 15)], s_g2)
    left(W.at[0, pl.ds(0, 3), :, A], s_w.at[0])
    left(W.at[0, pl.ds(0, 3), :, B], s_w.at[1])
    left(W.at[pl.ds(0, 3), :, :, A], s_w.at[2])
    left(W.at[pl.ds(0, 3), :, :, B], s_w.at[3])
    for i in range(3):
        left(TB, s_m.at[i])
    left(RY, s_y)
    left(RK, s_k)
    left(PC, s_r2)


def body(images, cotangent, depthwise_weight, norm_gain, norm_bias, up_weight):
    pixels = (
        images.shape[0] * images.shape[1] * images.shape[2]
        * lax.axis_size("shard") * lax.axis_size("rep")
    )
    factor = 1.0 / math.sqrt(pixels)
    dma = pltpu.SemaphoreType.DMA
    vm = lambda dtype, *shape: pltpu.VMEM(shape, dtype)
    shapes = (
        jax.ShapeDtypeStruct((8, 16, 768), BF16),
        jax.ShapeDtypeStruct((12, 1536), F32),
        jax.ShapeDtypeStruct((12, 49), F32),
        jax.ShapeDtypeStruct((1, 12), F32),
        jax.ShapeDtypeStruct((1, 12), F32),
    )
    results = pl.pallas_call(
        functools.partial(kernel, factor),
        out_shape=shapes,
        in_specs=[pl.BlockSpec(memory_space=pltpu.HBM)] * 6,
        out_specs=[pl.BlockSpec(memory_space=pltpu.VMEM)] * 5,
        scratch_shapes=[
            vm(BF16, 8, 16, 768),
            vm(BF16, 768, 768),
            vm(BF16, 8, 16, 768),
            vm(BF16, 12, 1536),
            vm(BF16, 12, 49),
            vm(BF16, 1, 12),
            vm(BF16, 1, 12),
            vm(F32, 16, 768),
            vm(F32, 12, 128),
            vm(BF16, 16, 768),
            vm(BF16, 15, 16, 768),
            vm(BF16, 4, 16, 768),
            vm(BF16, 4, 4, 48, 768),
            vm(BF16, 16, 24, 128),
            vm(F32, CH, 64, 128),
            vm(F32, CH, 8, 32, 128),
            vm(F32, CH, 8, 32, 128),
            vm(F32, CH, 8, 16, 128),
            vm(F32, 8, 16, 128),
            vm(BF16, 2, 128, 768),
            vm(BF16, 768, 256),
            vm(BF16, 2, 128, 768),
            vm(F32, 256, 768),
            vm(BF16, 2, 128, 768),
            vm(F32, 2, 128, 768),
            vm(F32, 128, 768),
            vm(F32, 4, 4, 48, 768),
            vm(BF16, 4, 4, 48, 768),
            vm(BF16, 4, 48, 768),
            vm(BF16, 4, 48, 768),
            vm(BF16, 4, 48, 768),
            vm(BF16, 4, 48, 768),
            vm(F32, 48, 768),
            vm(BF16, 4, 48, 768),
            vm(BF16, 7, 48, 384),
            vm(F32, 48, 384),
            vm(F32, CH, 128, 128),
            vm(F32, 768, 128),
            vm(F32, 16, 24, 128),
            vm(BF16, 16, 24, 128),
            vm(BF16, 15, 24, 128),
            vm(F32, 48, 128),
            vm(F32, 4, 16, 384),
            vm(BF16, 4, 16, 384),
            vm(BF16, 16, 16, 384),
            vm(BF16, 16, 384),
            vm(BF16, 16, 384),
            vm(BF16, 4, 16, 384),
            dma((6,)),
            dma, dma,
            dma, dma,
            dma((4,)), dma((4,)),
            dma((3,)), dma((3,)),
            dma((3,)), dma((4,)), dma((4,)), dma((4,)),
            dma, dma,
            dma, dma,
            dma, dma,
            dma, dma,
            dma, dma,
        ],
        compiler_params=pltpu.CompilerParams(
            collective_id=0, has_side_effects=True, vmem_limit_bytes=40 << 20
        ),
    )(
        *[
            pltpu.with_memory_space_constraint(v, pltpu.HBM)
            for v in (
                images.reshape(8, 16, 768), cotangent.reshape(128, 1536), depthwise_weight,
                norm_gain.reshape(1, 12), norm_bias.reshape(1, 12), up_weight,
            )
        ]
    )
    gi, gu, gd, gg, gb = pl.pallas_call(
        hand_over,
        out_shape=shapes,
        in_specs=[pl.BlockSpec(memory_space=pl.ANY)] * 5,
        out_specs=[pl.BlockSpec(memory_space=pltpu.HBM)] * 5,
        scratch_shapes=[dma((5,))],
        compiler_params=pltpu.CompilerParams(vmem_limit_bytes=1 << 20),
    )(*results)
    return (gi.reshape(images.shape), gu, gd, gg.reshape(12), gb.reshape(12))


def solution(mesh):
    placed = (
        P(("shard", "rep"), None, None, None),
        P(("shard", "rep"), None, None, None),
        P("shard", None),
        P("shard"),
        P("shard"),
        P("shard", None),
    )
    return jax.shard_map(
        body,
        mesh=mesh,
        in_specs=placed,
        out_specs=(
            P(("shard", "rep"), None, None, None),
            P("shard", None),
            P("shard", None),
            P("shard"),
            P("shard"),
        ),
        check_vma=False,
    )
```
